32 devices in a mesh: gx: 4 (over z), gy: 8 (over y, x, core).
Axes of the slice: x: 2, y: 2, z: 4, core: 2. Of those that a mesh axis runs over, the one named last changes fastest.
Arguments:
- point_feats: bfloat16 [512, 64, 128], P(('gx', 'gy')), may hold values from -6 to 6
- offsets: bfloat16 [512, 3, 128], P(('gx', 'gy')), may hold values from 0 to 1
- targets: int32 [512, 1], P(('gx', 'gy')), may hold values from 0 to 7; in each aligned block of 16 rows (0 to 15, 16 to 31, ...) at most 4 rows name the same one
- zstart: int32 [512], P(('gx', 'gy')), may hold values from 0 to 63
- enc_in: float32 [3, 64], replicated, may hold values from -4 to 4
- enc_bias: float32 [64], replicated, may hold values from -4 to 4
- enc_out: bfloat16 [64, 64], replicated, may hold values from -0.75 to 0.75
- dec_in: float32 [3, 64], replicated, may hold values from -4 to 4
- dec_bias: float32 [64], replicated, may hold values from -4 to 4
- dec_out: bfloat16 [64, 64], replicated, may hold values from -0.75 to 0.75
- spec_weight: float32 [32, 32, 32, 4096], P(None, 'gx', 'gy'), may hold values from -0.75 to 0.75
- local_weight: float32 [64, 64], replicated, may hold values from -0.75 to 0.75
- local_bias: float32 [64], replicated, may hold values from -3 to 3
- head_weight: float32 [64], replicated, may hold values from -4 to 4
Outputs:
- pressure: float32 [512, 128], P(('gx', 'gy'))
The draws below stay inside these ranges and needn't reach their ends.
Inputs may be any that keep to these rules, and one draw needn't show every extreme that they name: `targets`: A block's cells lie in the pencil of its own gx row with this gy index; at most 4 blocks of one device share a target, and exactly 4 do on some devices.
All inputs are finite; a program needn't handle non-finite values.
Results may differ from the reference program's by a relative error of at most 0.0014.
Values may be sent and summed in bfloat16 or wider, within the bound.
No kernel may reach another device: no remote copies, remote signals or barrier semaphores. Data moves between devices by JAX's collectives and lax.ppermute only.
A program may use at most 128 MiB of HBM per device.

```python
import math
import jax
import jax.numpy as jnp
import numpy as np
from jax import lax

C = 64
HK = 64
G = 64
M = 32
PB = 128
BD = 16
CAP = 4
NB = 512
N_GX = 4
N_GY = 8


def set_ends(drawn, rng, smallest, high):
    index_at = [jax.random.randint(jax.random.fold_in(rng, axis), (), 0, length) for axis, length in enumerate(drawn.shape)]
    widest = drawn.shape.index(max(drawn.shape))
    next_to = index_at[:widest] + [(index_at[widest] + 1) % drawn.shape[widest]] + index_at[widest + 1:]
    return drawn.at[tuple(index_at)].set(smallest).at[tuple(next_to)].set(high)


def block_levels(rng, shape, shards, least, top_value):
    def one(axis_at, parts):
        draws = jax.random.uniform(jax.random.fold_in(jax.random.fold_in(rng, 6), axis_at), (parts,), jnp.float32, least / len(shards), top_value / len(shards))
        return jnp.repeat(jnp.exp(draws), shape[axis_at] // parts).reshape((-1,) + (1,) * (len(shape) - axis_at - 1))

    loudness = one(*shards[0])
    for cut in shards[1:]:
        loudness = loudness * one(*cut)
    return loudness


def shared_out(own_key, own, number, rows, number_of, top, limit, skew):
    ranking = jax.random.permutation(own_key, number_of)
    heavy_load, ordinary = shares(number_of, rows * top, limit, skew, True), shares(number_of, rows * top, limit, skew, False)
    places = jnp.arange(number_of)

    def named(tallies, rotation):
        used = int((tallies > 0).sum())
        fixed = max(1, used // 4)
        moved = fixed + (places - fixed + rotation * (used - fixed)) % max(1, number_of - fixed)
        return jnp.zeros((number_of,), jnp.int32).at[ranking[jnp.where(places < fixed, places, moved)]].set(jnp.asarray(tallies, jnp.int32))

    tallies = jnp.where(number % 4 == 0, named(heavy_load, number // 4), named(ordinary, number - number // 4 - 1))
    mixed = jax.random.permutation(jax.random.fold_in(own, 3), number_of)
    source_of, taker = mixed[0:number_of // 2 * 2:2], mixed[1:number_of // 2 * 2:2]
    slack = jnp.minimum(tallies[source_of] - 1, limit - tallies[taker]) // 2
    slack = jnp.where((source_of == ranking[0]) | (taker == ranking[0]) | (tallies[taker] == 0), 0, jnp.maximum(slack, 0))
    moved = jax.random.randint(jax.random.fold_in(own, 4), (number_of // 2,), 0, 1 << 20) % (slack + 1)
    tallies = tallies.at[source_of].add(-moved).at[taker].add(moved)
    items = jnp.searchsorted(jnp.cumsum(tallies), jnp.arange(rows * top), side="right").astype(jnp.int32)
    grid = items.reshape(top, rows).T
    grid = grid[jax.random.permutation(jax.random.fold_in(own, 1), rows)]
    rotation = jax.random.randint(jax.random.fold_in(own, 2), (rows, 1), 0, top)
    return jnp.take_along_axis(grid, (jnp.arange(top)[None, :] + rotation) % top, axis=1)


def shares(number_of, total, limit, skew, full):
    portions = [(1 << 20) // math.isqrt(grade ** skew) + 1 for grade in range(1, number_of + 1)]
    largest = limit if full else min(limit, max(-(-total // number_of), total * portions[0] // sum(portions)))
    least = 1 if total - largest >= number_of - 1 else 0
    counts, spare = [largest] + [least] * (number_of - 1), total - largest - least * (number_of - 1)
    while spare > 0:
        candidates = [i for i in range(1, number_of) if counts[i] < largest] or [i for i in range(1, number_of) if counts[i] < limit]
        whole, budget = sum([portions[i] for i in candidates]), spare
        for i in candidates:
            more = min(limit - counts[i], max(1, budget * portions[i] // whole), spare)
            counts[i] = counts[i] + more
            spare = spare - more
    return np.array(counts)


def normal_values(key, shape, spread, most, shards=(), dtype=jnp.bfloat16):
    drawn = spread * jax.random.normal(key, shape, jnp.float32)
    if shards:
        drawn = drawn * block_levels(key, shape, shards, -0.22, 0.18)
    return jnp.clip(drawn, -most, most).astype(dtype)


def setup_inputs(seed: int = 0) -> dict:
    splits = jax.random.split(jax.random.key(seed), 15)
    point_feats = normal_values(splits[0], (NB, C, PB), 1.0, 6.0, ((0, 32),))
    offsets = jnp.clip(1.0 * jax.random.uniform(splits[1], (NB, 3, PB), jnp.float32) ** block_levels(splits[1], (NB, 3, PB), ((0, 32),), -0.2, 0.2), 0.0, 1.0).astype(jnp.bfloat16)
    targets_keys = jax.random.split(jax.random.fold_in(splits[2], 1), NB // BD)
    targets_turns = jax.random.permutation(jax.random.fold_in(splits[2], 3), NB // BD)
    targets = jax.vmap(lambda own, number: shared_out(jax.random.fold_in(splits[2], 2), own, number, BD, N_GY, 1, CAP, 1))(targets_keys, targets_turns).reshape((NB, 1))
    zstart = set_ends(jax.random.randint(splits[3], (NB,), 0, G), jax.random.fold_in(splits[3], 1), 0, G - 1).astype(jnp.int32)
    enc_in = normal_values(splits[4], (3, HK), 1.0, 4.0, (), jnp.float32)
    enc_bias = normal_values(splits[5], (HK,), 1.0, 4.0, (), jnp.float32)
    enc_out = normal_values(splits[6], (HK, C), HK ** -0.5, 0.75)
    dec_in = normal_values(splits[7], (3, HK), 1.0, 4.0, (), jnp.float32)
    dec_bias = normal_values(splits[8], (HK,), 1.0, 4.0, (), jnp.float32)
    dec_out = normal_values(splits[9], (HK, C), HK ** -0.5, 0.75)
    spec_weight = normal_values(splits[10], (M, M, M, C * C), C ** -0.5, 0.75, ((1, 4), (2, 8)), jnp.float32)
    local_weight = normal_values(splits[11], (C, C), C ** -0.5, 0.75, (), jnp.float32)
    local_bias = normal_values(splits[12], (C,), 0.5, 3.0, (), jnp.float32)
    head_weight = normal_values(splits[13], (C,), 1.0, 4.0, (), jnp.float32)
    return dict(point_feats=point_feats, offsets=offsets, targets=targets, zstart=zstart, enc_in=enc_in, enc_bias=enc_bias, enc_out=enc_out, dec_in=dec_in, dec_bias=dec_bias, dec_out=dec_out, spec_weight=spec_weight, local_weight=local_weight, local_bias=local_bias, head_weight=head_weight)


kernel_spread = 2.0
highest = lax.Precision.HIGHEST


def real_basis(length, modes):
    half = modes // 2
    places = jnp.arange(length).astype(jnp.float32)
    frequency = jnp.arange(half).astype(jnp.float32)
    angle_cos = 2.0 * jnp.pi * frequency[:, None] * places[None, :] / length
    angle_sin = 2.0 * jnp.pi * (frequency[:, None] + 1.0) * places[None, :] / length
    table = jnp.concatenate([jnp.cos(angle_cos), jnp.sin(angle_sin)], 0)
    return table * jnp.float32((2.0 / length) ** 0.5)


def tile_terms(offset_rows, weight_in, bias_in, cells_x, cells_y):
    cell_ids = jnp.arange(cells_x * cells_y)
    center_x = (cell_ids // cells_y).astype(jnp.float32) + 0.5
    center_y = (cell_ids % cells_y).astype(jnp.float32) + 0.5
    delta_x = (center_x[None, :, None] - cells_x * offset_rows[:, 0][:, None, :]) / kernel_spread
    delta_y = (center_y[None, :, None] - cells_y * offset_rows[:, 1][:, None, :]) / kernel_spread
    delta_z = (0.5 - offset_rows[:, 2][:, None, :]) / kernel_spread
    closeness = jnp.exp(-0.5 * (delta_x * delta_x + delta_y * delta_y + delta_z * delta_z))
    before = (delta_x[..., None] * weight_in[0] + delta_y[..., None] * weight_in[1]
              + delta_z[..., None] * weight_in[2] + bias_in)
    return (jax.nn.gelu(before, approximate=False) * closeness[..., None]).astype(jnp.bfloat16)


def encode(weighted, feats, out_weight):
    partial_sums = jnp.einsum('bcph,bop->bcho', weighted, feats, precision=highest)
    return jnp.einsum('bcho,ho->boc', partial_sums, out_weight, precision=highest) * (feats.shape[2] ** -0.5)


def decode(weighted, tile_values, out_weight):
    folded = (out_weight[None, None, :, :] * jnp.transpose(tile_values, (0, 2, 1))[:, :, None, :]).astype(jnp.bfloat16)
    return jnp.einsum('bcph,bcho->bop', weighted, folded.astype(jnp.float32),
                      precision=highest) * (weighted.shape[1] ** -0.5)


def reference(point_feats, offsets, targets, zstart, enc_in, enc_bias, enc_out, dec_in, dec_bias, dec_out,
              spec_weight, local_weight, local_bias, head_weight):
    cells_x = G // N_GX
    cells_y = G // N_GY
    tile_cells = cells_x * cells_y
    total = point_feats.shape[0]
    group_size = 32
    groups = total // group_size

    def encode_group(pieces):
        feats_group, offs_group = pieces
        weighted = tile_terms(offs_group.astype(jnp.float32), enc_in, enc_bias, cells_x, cells_y)
        return encode(weighted.astype(jnp.float32), feats_group.astype(jnp.float32), enc_out.astype(jnp.float32))

    contrib = lax.map(encode_group, (point_feats.reshape(groups, group_size, C, PB),
                                     offsets.reshape(groups, group_size, 3, PB)))
    contrib = contrib.reshape(total, C, tile_cells)

    block_ids = jnp.arange(total).astype(jnp.int32)
    row_index = (block_ids // BD) // N_GY
    column = targets[:, 0].astype(jnp.int32)
    cell_ids = jnp.arange(tile_cells).astype(jnp.int32)
    grid_x = row_index[:, None] * cells_x + cell_ids[None, :] // cells_y
    grid_y = column[:, None] * cells_y + cell_ids[None, :] % cells_y
    grid_z = zstart.astype(jnp.int32)[:, None] + 0 * cell_ids[None, :]
    cell_index = ((grid_x * G + grid_y) * G + grid_z).astype(jnp.int32).reshape(-1)
    flat_grid = jnp.zeros((G * G * G, C), jnp.float32).at[cell_index].add(
        jnp.transpose(contrib, (0, 2, 1)).reshape(-1, C))
    grid_cells = jnp.transpose(flat_grid.reshape(G, G, G, C), (3, 0, 1, 2))

    table = real_basis(G, M)
    spectrum = jnp.einsum('oxyz,kz->oxyk', grid_cells, table, precision=highest)
    spectrum = jnp.einsum('oxyk,ly->oxlk', spectrum, table, precision=highest)
    spectrum = jnp.einsum('oxlk,jx->ojlk', spectrum, table, precision=highest)
    mixed_modes = jnp.einsum('ojlk,jlkoq->qjlk', spectrum, spec_weight.reshape(M, M, M, C, C), precision=highest)
    returned = jnp.einsum('ojlk,jx->oxlk', mixed_modes, table, precision=highest)
    returned = jnp.einsum('oxlk,ly->oxyk', returned, table, precision=highest)
    returned = jnp.einsum('oxyk,kz->oxyz', returned, table, precision=highest)
    local_term = jnp.einsum('oxyz,oq->qxyz', grid_cells, local_weight, precision=highest) + local_bias[:, None, None, None]
    latent = jax.nn.gelu(returned + local_term, approximate=False).astype(jnp.bfloat16)

    tile_values = latent.reshape(C, -1)[:, cell_index].reshape(C, total, tile_cells)
    tile_values = jnp.transpose(tile_values, (1, 0, 2))

    def decode_group(pieces):
        tiles_group, offs_group = pieces
        weighted = tile_terms(offs_group.astype(jnp.float32), dec_in, dec_bias, cells_x, cells_y)
        values = decode(weighted.astype(jnp.float32), tiles_group.astype(jnp.float32), dec_out.astype(jnp.float32))
        return jnp.einsum('bop,o->bp', jax.nn.gelu(values, approximate=False), head_weight, precision=highest)

    pressure = lax.map(decode_group, (tile_values.reshape(groups, group_size, C, tile_cells),
                                      offsets.reshape(groups, group_size, 3, PB)))
    return pressure.reshape(total, PB)
```

```python
import functools

import jax
import jax.numpy as jnp
import numpy as np
from jax import lax
from jax.experimental import pallas as pl
from jax.experimental.pallas import tpu as pltpu
from jax.sharding import PartitionSpec as P

G = 64
M = 32
HALF = 0.5
ROOT = 0.5**0.5
f32 = jnp.float32
bf16 = jnp.bfloat16
PLANE_ROWS = 16
MODE_ROWS = 8


def real_basis(length, modes):
    half = modes // 2
    places = np.arange(length, dtype=np.float64)[None, :]
    frequency = np.arange(half, dtype=np.float64)[:, None]
    table = np.concatenate(
        [
            np.cos(2.0 * np.pi * frequency * places / length),
            np.sin(2.0 * np.pi * (frequency + 1.0) * places / length),
        ],
        0,
    )
    return table * (2.0 / length) ** 0.5


def two_parts(matrix):
    matrix = np.asarray(matrix, np.float32)
    high = matrix.astype(bf16)
    low = (matrix - high.astype(np.float32)).astype(bf16)
    return high, low


def dot(a, b):
    return jnp.dot(a, b, preferred_element_type=f32)


def dot_rows(a, b):
    return lax.dot_general(a, b, (((1,), (1,)), ((), ())), preferred_element_type=f32)


def vmem(count):
    return [pl.BlockSpec(memory_space=pltpu.VMEM) for _ in range(count)]


def lane_left(shape, half):
    return lax.broadcasted_iota(jnp.int32, shape, len(shape) - 1) < half


def weight_table(w_ref, b_ref, cx, cy):
    xr = cx // 2
    rows = max(8, xr)
    weights = jnp.concatenate([w_ref[...], b_ref[...]], 0) * ROOT
    count = weights.shape[1]
    columns = jnp.concatenate([weights, jnp.zeros_like(weights)], 0).T
    flat = (count, 128)
    wx, wy, wz, bias = [jnp.broadcast_to(columns[:, k : k + 1], flat) for k in range(4)]
    lane = lax.broadcasted_iota(jnp.int32, flat, 1)
    slope = jnp.where(lane < 3, wx * (-cx * HALF), jnp.where(lane < 6, wy * (-cy * HALF), wz * -HALF))
    fixed = jnp.where(lane < 9, slope, wz * (0.5 * HALF) + bias)
    along_x = jnp.where(lane < 9, 0.0, wx)
    along_y = jnp.where(lane < 9, 0.0, wy)
    shape = (count, rows, 128)
    row = lax.broadcasted_iota(jnp.int32, shape, 1)
    lane = lax.broadcasted_iota(jnp.int32, shape, 2)
    at_x = ((row % xr).astype(f32) + 0.5) * HALF
    at_y = ((row // xr).astype(f32) + 0.5) * HALF
    value = fixed[:, None, :] + (at_x * along_x[:, None, :] + at_y * along_y[:, None, :])
    high = value.astype(bf16).astype(f32)
    middle = (value - high).astype(bf16).astype(f32)
    low = value - high - middle
    part = lane % 3
    table = jnp.where(part == 0, high, jnp.where(part == 1, middle, low))
    return jnp.where(lane < 12, table, 0.0).astype(bf16).reshape(count * rows, 128)


def tile_geometry(offset_rows, table, cx, cy, near_ref, base_ref):
    xr = cx // 2
    gj = max(1, 8 // xr)
    rows = gj * xr
    points = offset_rows.shape[1]
    one = jnp.ones((3, points), f32)
    parts = [offset_rows[k : k + 1] for k in range(3) for _ in range(3)] + [one]
    parts = parts + [jnp.zeros((128 - 12, points), f32)]
    base_ref[...] = dot(table, jnp.concatenate(parts, 0).astype(bf16))
    row = lax.broadcasted_iota(jnp.int32, (rows, points), 0)
    dx = ((row % xr).astype(f32) + 0.5 - cx * offset_rows[0:1]) * HALF
    dy = ((row // xr).astype(f32) + 0.5 - cy * offset_rows[1:2]) * HALF
    dz = (0.5 - offset_rows[2:3]) * HALF
    for side in range(2):
        dxs = dx + side * xr * HALF
        for group in range(cy // gj):
            dys = dy + group * gj * HALF
            start = (side * (cy // gj) + group) * rows
            near = jnp.exp(-0.5 * (dxs * dxs + dys * dys + dz * dz)) * ROOT
            near_ref[start : start + rows, :] = near


def hidden(near_ref, base_ref, w_ref, h, cx, cy):
    xr = cx // 2
    gj = max(1, 8 // xr)
    rows = gj * xr
    base = base_ref[pl.ds(pl.multiple_of(h * rows, rows), rows), :]
    step = jnp.full(base.shape, w_ref[1, h] * (gj * HALF * ROOT), f32)
    places = []
    for side in range(2):
        place = base if side == 0 else base + w_ref[0, h] * (xr * HALF * ROOT)
        for group in range(cy // gj):
            if group:
                place = place + step
            places.append(place)
    u = jnp.concatenate(places, 0)
    t = u * near_ref[...]
    return (t + t * lax.erf(u)).astype(bf16)


def offset_rows(offs_ref, block):
    return jnp.concatenate([offs_ref[a, pl.ds(block, 1), :] for a in range(3)], 0)


def encoder_body(
    cx, cy, cap, t_ref, z_ref, ws_ref, w_ref, b_ref, offs_ref, feats_ref, out_w_ref,
    pay_ref, slot_ref, places_ref, table_ref, wrow_ref, rhs_ref, near_ref, base_ref, even_ref, odd_ref,
):
    step = pl.program_id(0)
    blocks = t_ref.shape[0]
    cells = cx * cy
    rows = cells // 2
    channels, points = feats_ref.shape[1:]
    lanes = 2 * channels
    group = even_ref.shape[0]
    count = wrow_ref.shape[0] * group

    @pl.when(step == 0)
    def _():
        pay_ref[...] = jnp.zeros(pay_ref.shape, bf16)
        rhs_ref[...] = jnp.zeros(rhs_ref.shape, bf16)
        places_ref[...] = offs_ref[...].astype(f32)
        table_ref[...] = weight_table(w_ref, b_ref, cx, cy)
        out_w = out_w_ref[...].astype(f32)
        wrow_ref[...] = jnp.concatenate([out_w, out_w], 1).reshape(wrow_ref.shape)
        row = lax.broadcasted_iota(jnp.int32, (PLANE_ROWS, lanes), 0)
        for b in range(blocks):
            target = t_ref[b]
            rank = jnp.int32(0)
            for other in range(b):
                rank = rank + (t_ref[other] == target).astype(jnp.int32)
            slot_ref[b] = target * cap + rank
            here = pl.ds(cap * rows, PLANE_ROWS)
            old = pay_ref[target, here, :].astype(f32)
            pay_ref[target, here, :] = jnp.where(row == rank, z_ref[b].astype(f32), old).astype(bf16)

    for q in range(2):
        rhs_ref[q * channels : (q + 1) * channels, q * points : (q + 1) * points] = feats_ref[q]
        offset = offset_rows(places_ref, 2 * step + q)
        tile_geometry(offset, table_ref[...], cx, cy, near_ref.at[q], base_ref.at[q])

    def fill(ref, first):
        for i in range(group):
            for q in range(2):
                ref[i, q] = hidden(near_ref.at[q], base_ref.at[q], ws_ref, first + i, cx, cy)

    def drain(ref, index, total):
        left = jnp.concatenate([ref[:, q].reshape(group * cells, points) for q in range(2)], 1)
        out = dot_rows(left, rhs_ref[...])
        weights = wrow_ref[index]
        for i in range(group):
            total = total + out[i * cells : (i + 1) * cells] * weights[i : i + 1]
        return total

    def one(index, total):
        first = 2 * index * group
        fill(odd_ref, first + group)
        total = drain(even_ref, 2 * index, total)
        fill(even_ref, first + 2 * group)
        return drain(odd_ref, 2 * index + 1, total)

    pairs = count // group // 2
    fill(even_ref, 0)
    total = lax.fori_loop(0, pairs - 1, one, jnp.zeros((cells, lanes), f32))
    fill(odd_ref, count - group)
    total = drain(even_ref, 2 * pairs - 2, total)
    total = drain(odd_ref, 2 * pairs - 1, total)
    total = total * points**-0.5
    top, bottom = total[:rows], total[rows:]
    left = lane_left((rows, lanes), channels)
    made = (
        jnp.where(left, top, pltpu.roll(bottom, channels, 1)),
        jnp.where(left, pltpu.roll(top, channels, 1), bottom),
    )
    for q in range(2):
        slot = slot_ref[2 * step + q]
        target = slot // cap
        start = pl.multiple_of((slot - target * cap) * rows, rows)
        pay_ref[target, pl.ds(start, rows), :] = made[q].astype(bf16)


def encoder(targets, zstart, weight_in, bias_in, offsets, feats, out_weight, cx, cy, ny, cap):
    blocks, channels, points = feats.shape
    cells = cx * cy
    rows = cells // 2
    count = out_weight.shape[0]
    group = 8
    smem = pl.BlockSpec(memory_space=pltpu.SMEM)
    full = lambda a: pl.BlockSpec(a.shape, lambda i: (0,) * a.ndim)
    payload = (ny, cap * rows + PLANE_ROWS, 2 * channels)
    base_rows = count * max(8, cx // 2)
    return pl.pallas_call(
        functools.partial(encoder_body, cx, cy, cap),
        grid=(blocks // 2,),
        in_specs=[
            smem,
            smem,
            smem,
            full(weight_in),
            full(bias_in),
            full(offsets),
            pl.BlockSpec((2, channels, points), lambda i: (i, 0, 0)),
            full(out_weight),
        ],
        out_specs=[pl.BlockSpec(payload, lambda i: (0, 0, 0)), smem],
        out_shape=[
            jax.ShapeDtypeStruct(payload, bf16),
            jax.ShapeDtypeStruct((blocks,), jnp.int32),
        ],
        scratch_shapes=[
            pltpu.VMEM(offsets.shape, f32),
            pltpu.VMEM((base_rows, 128), bf16),
            pltpu.VMEM((count // group, group, 2 * channels), f32),
            pltpu.VMEM((2 * channels, 2 * points), bf16),
            pltpu.VMEM((2, cells, points), f32),
            pltpu.VMEM((2, base_rows, points), f32),
            pltpu.VMEM((group, 2, cells, points), bf16),
            pltpu.VMEM((group, 2, cells, points), bf16),
        ],
        name="encoder",
    )(targets, zstart, weight_in, weight_in, bias_in, offsets, feats, out_weight)


def plane_onehot(planes, cap, width):
    spread, lanes = planes.shape
    slots = spread // PLANE_ROWS * cap
    shape = (slots * width, spread)
    slot = lax.broadcasted_iota(jnp.int32, shape, 0) // width
    source = (slot // cap) * PLANE_ROWS + slot % cap
    pick = (source == lax.broadcasted_iota(jnp.int32, shape, 1)).astype(f32).astype(bf16)
    rows = dot(pick, planes)
    place = lax.broadcasted_iota(jnp.int32, rows.shape, 1).astype(f32)
    return (rows == place).astype(f32).astype(bf16)


def same_row(shape, width):
    return lax.broadcasted_iota(jnp.int32, shape, 0) % width == lax.broadcasted_iota(jnp.int32, shape, 1) % width


def slot_rows(got_ref, cap, rows, group, width):
    parts = []
    for source in range(got_ref.shape[0]):
        for q in range(cap):
            parts.append(got_ref[source, q * rows + group * width : q * rows + (group + 1) * width, :])
    return jnp.concatenate(parts, 0)


def depth_body(cap, rows, width, got_ref, high_ref, low_ref, out_ref):
    lanes = got_ref.shape[2]
    planes = got_ref[:, cap * rows :, :].reshape(-1, lanes)
    onehot = plane_onehot(planes, cap, width)
    shape = (high_ref.shape[0], onehot.shape[0])
    same = same_row(shape, width)
    high = jnp.where(same, dot_rows(high_ref[...], onehot), 0.0).astype(bf16)
    low = jnp.where(same, dot_rows(low_ref[...], onehot), 0.0).astype(bf16)
    modes = out_ref.shape[0]
    for group in range(rows // width):
        right = slot_rows(got_ref, cap, rows, group, width)
        out = dot(high, right) + dot(low, right)
        out_ref[:, group * width : (group + 1) * width, :] = out.astype(bf16).reshape(modes, width, lanes)


def depth(got, table_rows, rows, cap, width):
    lanes = got.shape[2]
    return pl.pallas_call(
        functools.partial(depth_body, cap, rows, width),
        in_specs=vmem(3),
        out_specs=vmem(1)[0],
        out_shape=jax.ShapeDtypeStruct((M, rows, lanes), bf16),
        name="depth_forward",
    )(got, *table_rows)


def skip_body(cap, rows, width, got_ref, weight_ref, bias_ref, out_ref):
    lanes = got_ref.shape[2]
    weight = weight_ref[...]
    zero = jnp.zeros_like(weight)
    pair = jnp.concatenate(
        [jnp.concatenate([weight, zero], 1), jnp.concatenate([zero, weight], 1)], 0
    )
    pair_high = pair.astype(bf16)
    pair_low = (pair - pair_high.astype(f32)).astype(bf16)
    bias = jnp.concatenate([bias_ref[...], bias_ref[...]], 1)
    planes = got_ref[:, cap * rows :, :].reshape(-1, lanes)
    onehot = plane_onehot(planes, cap, width)
    size = onehot.shape[0]
    same = same_row((size, size), width)
    shared = jnp.where(same, dot_rows(onehot, onehot), 0.0).astype(bf16)
    for group in range(rows // width):
        cells = dot(shared, slot_rows(got_ref, cap, rows, group, width))
        high = cells.astype(bf16)
        low = (cells - high.astype(f32)).astype(bf16)
        term = dot(high, pair_high) + dot(low, pair_high) + dot(high, pair_low) + bias
        out_ref[:, group * width : (group + 1) * width, :] = term.reshape(size // width, width, lanes)


def skip(got, weight, bias, rows, cap, width):
    lanes = got.shape[2]
    slots = got.shape[0] * cap
    return pl.pallas_call(
        functools.partial(skip_body, cap, rows, width),
        in_specs=vmem(3),
        out_specs=vmem(1)[0],
        out_shape=jax.ShapeDtypeStruct((slots, rows, lanes), f32),
        name="skip",
    )(got, weight, bias)


def rows_of(ref, lead, start, size):
    if size % 16 == 0:
        return ref[lead, start : start + size, :]
    return ref[lead].astype(f32)[start : start + size]


def partner(me, d, count):
    if count & (count - 1) == 0:
        return me ^ d
    return (me + d) % count


def swap_pieces(pieces, axis):
    count = len(pieces)
    moved = [pieces[0]]
    for d in range(1, count):
        pairs = [(i, partner(i, d, count)) for i in range(count)]
        moved.append(lax.ppermute(pieces[d], axis, pairs))
    return moved


def source(me, d, count):
    if count & (count - 1) == 0:
        return me ^ d
    return (me + count - d) % count


def width_body(kb, xr, nx, me_ref, in_ref, high_ref, low_ref, *rest):
    out_refs, scratch = rest[:nx], rest[nx]
    ny, total, lanes = in_ref.shape
    rows = total // kb
    inner = kb * xr
    for k in range(kb):
        right = jnp.concatenate([in_ref[y, k * rows : (k + 1) * rows, :] for y in range(ny)], 0)
        out = dot(high_ref[...], right) + dot(low_ref[...], right)
        for e in range(M):
            scratch[e * inner + k * xr : e * inner + (k + 1) * xr, :] = out[e * xr : (e + 1) * xr]
    size = M * inner // nx
    for d in range(nx):
        start = pl.multiple_of(partner(me_ref[0], d, nx) * size, size)
        out_refs[d][...] = scratch[pl.ds(start, size), :].astype(bf16)


def width_forward(me, data, table, nx, kb, xr):
    lanes = data.shape[2]
    size = M * kb * xr
    return pl.pallas_call(
        functools.partial(width_body, kb, xr, nx),
        in_specs=[pl.BlockSpec(memory_space=pltpu.SMEM)] + vmem(3),
        out_specs=vmem(nx),
        out_shape=[jax.ShapeDtypeStruct((size // nx, lanes), bf16)] * nx,
        scratch_shapes=[pltpu.VMEM((size, lanes), f32)],
        name="width_forward",
    )(me, data, *table)


def mix_body(kb, nx, me_ref, *rest):
    in_refs = rest[:nx]
    spec_ref, forward_ref, high_ref, low_ref = rest[nx : nx + 4]
    out_refs = rest[nx + 4 : 2 * nx + 4]
    pick_ref, right_ref, back_ref = rest[2 * nx + 4 :]
    lanes = in_refs[0].shape[1]
    channels = lanes // 2
    fold = MODE_ROWS // kb
    half = fold * channels

    @pl.when(pl.program_id(0) == 0)
    def _():
        shape = pick_ref.shape[1:]
        row = lax.broadcasted_iota(jnp.int32, shape, 0) % half
        lane = lax.broadcasted_iota(jnp.int32, shape, 1)
        wanted = row % channels - 2 * (row // channels) - (lane % lanes) // channels
        wanted = wanted - 2 * fold * (lane // lanes)
        for v in range(pick_ref.shape[0]):
            pick_ref[v] = (wanted == 2 * fold * v * (shape[1] // lanes)).astype(f32).astype(bf16)

    each = spec_ref.shape[1]
    inner = in_refs[0].shape[0] // each
    right = []
    for e in range(each):
        rows = slice(e * inner, (e + 1) * inner)
        for d in range(nx):
            start = pl.multiple_of(source(me_ref[0], d, nx) * inner, inner)
            right_ref[e, pl.ds(start, inner), :] = in_refs[d][rows, :].astype(f32)
        right.append(right_ref[e].astype(bf16))
    right = jnp.concatenate(right, 1)
    out = dot(forward_ref[...], jnp.concatenate([right, right], 0))
    size = M * MODE_ROWS
    left = lane_left((size, lanes), channels)
    place = (lax.broadcasted_iota(jnp.int32, (size, lanes), 0) % MODE_ROWS) // kb
    side = lax.broadcasted_iota(jnp.int32, (size, lanes), 1) // channels
    masks = [place == 2 * pair + side for pair in range(fold // 2)]
    modes = []
    for e in range(each):
        here = out[:, e * lanes : (e + 1) * lanes]
        halves = jnp.where(left, here[:size], here[size:])
        halves = halves + pltpu.roll(halves, channels, 1)
        high = halves.astype(bf16).astype(f32)
        low = halves - high
        parts = [jnp.where(mask, part, 0.0) for part in (high, low) for mask in masks]
        modes.append(jnp.concatenate(parts, 1).astype(bf16))
    modes = jnp.concatenate(modes, 0)
    totals = [jnp.zeros((M, MODE_ROWS, lanes), f32) for e in range(each)]
    width = pick_ref.shape[2] // lanes
    for v in range(pick_ref.shape[0]):
        spread = dot(modes, pick_ref[v])
        for w in range(width):
            start = (v * width + w) * MODE_ROWS
            for e in range(each):
                part = spread[e * size : (e + 1) * size, w * lanes : (w + 1) * lanes]
                part = part.reshape(M, MODE_ROWS, lanes)
                totals[e] = totals[e] + part * spec_ref[:, e, start : start + MODE_ROWS, :]
    mixed = jnp.concatenate([total.reshape(size, lanes) for total in totals], 1)
    high = mixed.astype(bf16)
    low = (mixed - high.astype(f32)).astype(bf16)
    back = dot(high_ref[...], high) + dot(high_ref[...], low) + dot(low_ref[...], high)
    count = nx * inner
    left = lane_left((count, lanes), channels)
    for e in range(each):
        here = back[:, e * lanes : (e + 1) * lanes]
        here = here + pltpu.roll(here, channels, 1)
        back_ref[e] = jnp.where(left, here[:count], here[count:])
        for d in range(nx):
            start = pl.multiple_of(partner(me_ref[0], d, nx) * inner, inner)
            out_refs[d][e * inner : (e + 1) * inner, :] = back_ref[e, pl.ds(start, inner), :].astype(bf16)


def mix(me, pieces, spec, forward, inverse, inner):
    nx = len(pieces)
    total, lanes = pieces[0].shape
    eb, kb, wide = spec.shape[1:]
    chunks = wide // lanes
    spec = spec.reshape(M, eb, kb, chunks, lanes).transpose(0, 1, 3, 2, 4).reshape(M, eb, chunks * kb, lanes)
    full = lambda a: pl.BlockSpec(a.shape, lambda e: (0,) * a.ndim)
    each = 2 if eb % 2 == 0 else 1
    piece = pl.BlockSpec((each * inner, lanes), lambda e: (e, 0))
    fold = MODE_ROWS // kb
    return pl.pallas_call(
        functools.partial(mix_body, kb, nx),
        grid=(eb // each,),
        in_specs=[pl.BlockSpec(memory_space=pltpu.SMEM)]
        + [piece] * nx
        + [
            pl.BlockSpec((M, each) + spec.shape[2:], lambda e: (0, e, 0, 0)),
            full(forward),
            full(inverse[0]),
            full(inverse[1]),
        ],
        out_specs=[piece] * nx,
        out_shape=[jax.ShapeDtypeStruct((total, lanes), bf16)] * nx,
        scratch_shapes=[
            pltpu.VMEM((chunks // fold // 2, fold * lanes, 2 * lanes), bf16),
            pltpu.VMEM((each, nx * inner, lanes), f32),
            pltpu.VMEM((each, nx * inner, lanes), f32),
        ],
        name="mix",
    )(me, *pieces, spec, forward, *inverse)


def width_back_body(kb, xr, nx, me_ref, *rest):
    in_refs = rest[:nx]
    high_ref, low_ref, out_ref, right_ref, made_ref = rest[nx:]
    total, lanes = in_refs[0].shape
    ny = out_ref.shape[0]
    inner = kb * xr
    for d in range(nx):
        start = pl.multiple_of(source(me_ref[0], d, nx) * total, total)
        right_ref[pl.ds(start, total), :] = in_refs[d][...].astype(f32)
    for k in range(kb):
        right = jnp.concatenate(
            [right_ref[e * inner + k * xr : e * inner + (k + 1) * xr, :] for e in range(M)], 0
        ).astype(bf16)
        out = dot(high_ref[...], right) + dot(low_ref[...], right)
        for y in range(G):
            made_ref[y * inner + k * xr : y * inner + (k + 1) * xr, :] = out[y * xr : (y + 1) * xr]
    out_ref[...] = made_ref[...].astype(bf16).reshape(out_ref.shape)


def width_back(me, pieces, table, ny, kb, xr):
    nx = len(pieces)
    lanes = pieces[0].shape[1]
    inner = kb * xr
    return pl.pallas_call(
        functools.partial(width_back_body, kb, xr, nx),
        in_specs=[pl.BlockSpec(memory_space=pltpu.SMEM)] + vmem(nx + 2),
        out_specs=vmem(1)[0],
        out_shape=jax.ShapeDtypeStruct((ny, G // ny * inner, lanes), bf16),
        scratch_shapes=[pltpu.VMEM((M * inner, lanes), f32), pltpu.VMEM((G * inner, lanes), f32)],
        name="width_back",
    )(me, *pieces, *table)


def latent_body(cap, inner, xr, in_ref, planes_ref, skip_ref, high_ref, low_ref, out_ref, scratch):
    ny, total, lanes = in_ref.shape
    slots = skip_ref.shape[0]
    onehot = plane_onehot(planes_ref[...].reshape(-1, lanes), cap, xr)
    shape = (onehot.shape[0], high_ref.shape[0])
    same = same_row(shape, xr)
    high = jnp.where(same, dot_rows(onehot, high_ref[...]), 0.0).astype(bf16)
    low = jnp.where(same, dot_rows(onehot, low_ref[...]), 0.0).astype(bf16)
    for j in range(total // inner):
        right = jnp.concatenate([rows_of(in_ref, t, j * inner, inner) for t in range(ny)], 0).astype(bf16)
        out = (dot(high, right) + dot(low, right)).reshape(slots, xr, lanes)
        here = slice(j * xr, (j + 1) * xr)
        out = out + skip_ref[:, here, :]
        scratch[:, here, :] = 0.5 * out * (1.0 + lax.erf(out * ROOT))
    out_ref[...] = scratch[...].astype(bf16)


def latent_tiles(data, got, skipped, table_rows, cap, rows, inner, xr):
    ny, _, lanes = data.shape
    full = lambda a: pl.BlockSpec(a.shape, lambda i: (0,) * a.ndim)
    return pl.pallas_call(
        functools.partial(latent_body, cap, inner, xr),
        grid=(1,),
        in_specs=[
            full(data),
            pl.BlockSpec((ny, PLANE_ROWS, lanes), lambda i: (0, cap * rows // PLANE_ROWS, 0)),
            full(skipped),
            full(table_rows[0]),
            full(table_rows[1]),
        ],
        out_specs=pl.BlockSpec(skipped.shape, lambda i: (0, 0, 0)),
        out_shape=jax.ShapeDtypeStruct(skipped.shape, bf16),
        scratch_shapes=[pltpu.VMEM(skipped.shape, f32)],
        name="latent",
    )(data, got, skipped, *table_rows)


STEP = 2


def spread_body(out_w_ref, head_ref, wcol_ref, wide_ref):
    count, channels, cells = wcol_ref.shape
    columns = out_w_ref[...].astype(f32).T
    for h in range(count):
        wcol_ref[h] = jnp.broadcast_to(columns[:, h : h + 1], (channels, cells)).astype(bf16)
    wide_ref[...] = jnp.broadcast_to(head_ref[...], (wide_ref.shape[1], channels)).T


def spread(out_weight, head, cells, points):
    count, channels = out_weight.shape
    return pl.pallas_call(
        spread_body,
        in_specs=vmem(2),
        out_specs=vmem(2),
        out_shape=[
            jax.ShapeDtypeStruct((count, channels, cells), bf16),
            jax.ShapeDtypeStruct((channels, points), f32),
        ],
        name="spread",
    )(out_weight, head)


def ahead_body(cx, cy, group, first, ws_ref, w_ref, b_ref, offs_ref, *rest):
    hidden_ref, places_ref, table_ref, near_ref, base_ref = rest[-5:]
    cells = cx * cy
    step = pl.program_id(0)

    @pl.when(step == 0)
    def _():
        places_ref[...] = offs_ref[...].astype(f32)
        table_ref[...] = weight_table(w_ref, b_ref, cx, cy)

    tile_geometry(offset_rows(places_ref, step + first), table_ref[...], cx, cy, near_ref, base_ref)

    def one(index, carry):
        for i in range(group):
            h = index * group + i
            start = pl.multiple_of(h * cells, cells)
            hidden_ref[0, pl.ds(start, cells), :] = hidden(near_ref, base_ref, ws_ref, h, cx, cy)
        return carry

    lax.fori_loop(0, b_ref.shape[1] // group, one, 0)


def ahead(weight_in, bias_in, offsets, cx, cy, first, number, old):
    _, blocks, points = offsets.shape
    cells = cx * cy
    count = bias_in.shape[1]
    full = lambda a: pl.BlockSpec(a.shape, lambda i: (0,) * a.ndim)
    made = (blocks, count * cells, points)
    base_rows = count * max(8, cx // 2)
    return pl.pallas_call(
        functools.partial(ahead_body, cx, cy, 16, first),
        grid=(number,),
        in_specs=[pl.BlockSpec(memory_space=pltpu.SMEM), full(weight_in), full(bias_in), full(offsets)]
        + [pl.BlockSpec(memory_space=pl.ANY)] * len(old),
        out_specs=pl.BlockSpec((1,) + made[1:], lambda i: (i + first, 0, 0)),
        out_shape=jax.ShapeDtypeStruct(made, bf16),
        scratch_shapes=[
            pltpu.VMEM(offsets.shape, f32),
            pltpu.VMEM((base_rows, 128), bf16),
            pltpu.VMEM((cells, points), f32),
            pltpu.VMEM((base_rows, points), f32),
        ],
        input_output_aliases={4: 0} if old else {},
        name="ahead",
    )(weight_in, weight_in, bias_in, offsets, *old)


def decoder_body(cells, group, slot_ref, *rest):
    tile_refs = rest[:STEP]
    ready_ref, wcol_ref, wide_ref, out_ref = rest[STEP:]
    step = pl.program_id(0)
    count, channels, _ = wcol_ref.shape
    points = ready_ref.shape[2]

    def tile_of(ref):
        tile = ref[0].astype(f32).T
        return jnp.concatenate([tile[:channels], tile[channels:]], 1).astype(bf16)

    tiles = [tile_of(ref) for ref in tile_refs]

    def one(index, totals):
        first = index * group
        start = pl.multiple_of(first * cells, group * cells)
        out = []
        for q in range(STEP):
            folded = jnp.concatenate([tiles[q] * wcol_ref[first + i] for i in range(group)], 1)
            out.append(totals[q] + dot(folded, ready_ref[q, pl.ds(start, group * cells), :]))
        return tuple(out)

    zero = jnp.zeros((channels, points), f32)
    totals = lax.fori_loop(0, count // group, one, (zero,) * STEP)
    for q in range(STEP):
        values = totals[q] * cells**-0.5
        active = 0.5 * values * (1.0 + lax.erf(values * ROOT))
        row = jnp.sum(active * wide_ref[...], axis=0, keepdims=True)
        out_ref[pl.ds(STEP * step + q, 1), :] = row


def decoder(slots, tiles, ready, wcol, wide, cells):
    blocks, _, points = ready.shape
    group = 16
    full = lambda a: pl.BlockSpec(a.shape, lambda b, s: (0,) * a.ndim)
    tile = (1,) + tiles.shape[1:]

    def tile_spec(q):
        return pl.BlockSpec(tile, lambda b, s: (s[STEP * b + q], 0, 0))

    return pl.pallas_call(
        functools.partial(decoder_body, cells, group),
        grid_spec=pltpu.PrefetchScalarGridSpec(
            num_scalar_prefetch=1,
            grid=(blocks // STEP,),
            in_specs=[tile_spec(q) for q in range(STEP)]
            + [
                pl.BlockSpec((STEP,) + ready.shape[1:], lambda b, s: (b, 0, 0)),
                full(wcol),
                full(wide),
            ],
            out_specs=pl.BlockSpec((blocks, points), lambda b, s: (0, 0)),
        ),
        out_shape=jax.ShapeDtypeStruct((blocks, points), f32),
        name="decoder",
    )(slots, *([tiles] * STEP), ready, wcol, wide)


def local(
    point_feats,
    offsets,
    targets,
    zstart,
    enc_in,
    enc_bias,
    enc_out,
    dec_in,
    dec_bias,
    dec_out,
    spec_weight,
    local_weight,
    local_bias,
    head_weight,
):
    nx = lax.axis_size("gx")
    ny = lax.axis_size("gy")
    cx = G // nx
    cy = G // ny
    rows = cx * cy // 2
    xr = cx // 2
    kb = M // ny
    inner = kb * xr
    blocks, channels, points = point_feats.shape
    lanes = 2 * channels
    cap = max(2, 2 * blocks // ny)
    fold = MODE_ROWS // kb

    table = real_basis(G, M)
    eye = np.eye
    depth_table = np.zeros((M, lanes))
    depth_table[:, :G] = table
    depth_rows = two_parts(np.repeat(depth_table, 16, 0))
    depth_back_rows = two_parts(np.repeat(depth_table, xr, 0))
    width_table = two_parts(np.kron(table, eye(xr)))
    width_back_table = two_parts(np.kron(table.T, eye(xr)))
    by_x = table.reshape(M, nx, 2, xr)
    copies = np.tile(eye(kb), (fold, 1))
    length_table = np.einsum("aBvr,fk->vafBkr", by_x, copies).reshape(2 * M * MODE_ROWS, nx * inner)
    length_forward = np.concatenate(two_parts(length_table), 1)
    length_back = two_parts(
        np.einsum("aBvr,fk->vBkraf", by_x, copies).reshape(2 * nx * inner, M * MODE_ROWS)
    )

    swap = functools.partial(lax.all_to_all, split_axis=0, concat_axis=0, tiled=True)
    me = lax.axis_index("gx").astype(jnp.int32).reshape(1)
    offs = jnp.transpose(offsets, (1, 0, 2))

    payload, slots = encoder(
        targets[:, 0], zstart, enc_in, enc_bias[None, :], offs, point_feats, enc_out, cx, cy, ny, cap
    )
    third = blocks // 3
    made = functools.partial(ahead, dec_in, dec_bias[None, :], offs, cx, cy)
    got = swap(payload, "gy")
    ready = made(0, third, ())
    got, ready = lax.optimization_barrier((got, ready))
    data = depth(got, depth_rows, rows, cap, 16)
    ready = made(third, third, (ready,))
    data = swap(data.reshape(ny, kb * rows, lanes), "gy")
    data, ready = lax.optimization_barrier((data, ready))
    wcol, wide = spread(dec_out, head_weight[None, :], cx * cy, points)
    skipped = skip(got, local_weight, local_bias[None, :], rows, cap, 16)
    pieces = width_forward(me, data, width_table, nx, kb, xr)
    pieces = swap_pieces(pieces, "gx")
    pieces = mix(me, pieces, spec_weight, length_forward, length_back, inner)
    pieces = swap_pieces(pieces, "gx")
    data = width_back(me, pieces, width_back_table, ny, kb, xr)
    data = swap(data, "gy")
    data, skipped, wcol, wide = lax.optimization_barrier((data, skipped, wcol, wide))
    tiles = latent_tiles(data, got, skipped, depth_back_rows, cap, rows, inner, xr)
    ready = made(2 * third, blocks - 2 * third, (ready,))
    tiles = swap(tiles.reshape(ny, cap * rows, lanes), "gy")
    tiles = tiles.reshape(ny * cap, rows, lanes)
    return decoder(slots, tiles, ready, wcol, wide, cx * cy)


def solution(mesh):
    placed = (
        P(("gx", "gy"), None, None),
        P(("gx", "gy"), None, None),
        P(("gx", "gy"), None),
        P(("gx", "gy")),
        P(),
        P(),
        P(),
        P(),
        P(),
        P(),
        P(None, "gx", "gy", None),
        P(),
        P(),
        P(),
    )
    return jax.shard_map(
        local, mesh=mesh, in_specs=placed, out_specs=P(("gx", "gy"), None), check_vma=False
    )
```

```python
import functools

import jax
import jax.numpy as jnp
import numpy as np
from jax import lax
from jax.experimental import pallas as pl
from jax.experimental.pallas import tpu as pltpu
from jax.sharding import PartitionSpec as P

G = 64
M = 32
HALF = 0.5
ROOT = 0.5**0.5
f32 = jnp.float32
bf16 = jnp.bfloat16
PLANE_ROWS = 16
MODE_ROWS = 8


def real_basis(length, modes):
    half = modes // 2
    places = np.arange(length, dtype=np.float64)[None, :]
    frequency = np.arange(half, dtype=np.float64)[:, None]
    table = np.concatenate(
        [
            np.cos(2.0 * np.pi * frequency * places / length),
            np.sin(2.0 * np.pi * (frequency + 1.0) * places / length),
        ],
        0,
    )
    return table * (2.0 / length) ** 0.5


def two_parts(matrix):
    matrix = np.asarray(matrix, np.float32)
    high = matrix.astype(bf16)
    low = (matrix - high.astype(np.float32)).astype(bf16)
    return high, low


def dot(a, b):
    return jnp.dot(a, b, preferred_element_type=f32)


def dot_rows(a, b):
    return lax.dot_general(a, b, (((1,), (1,)), ((), ())), preferred_element_type=f32)


def vmem(count):
    return [pl.BlockSpec(memory_space=pltpu.VMEM) for _ in range(count)]


def near(array):
    return pltpu.with_memory_space_constraint(array, pltpu.MemorySpace.VMEM)


def lane_left(shape, half):
    return lax.broadcasted_iota(jnp.int32, shape, len(shape) - 1) < half


def weight_table(w_ref, b_ref, cx, cy):
    xr = cx // 2
    rows = max(8, xr)
    weights = jnp.concatenate([w_ref[...], b_ref[...]], 0) * ROOT
    count = weights.shape[1]
    columns = jnp.concatenate([weights, jnp.zeros_like(weights)], 0).T
    flat = (count, 128)
    wx, wy, wz, bias = [jnp.broadcast_to(columns[:, k : k + 1], flat) for k in range(4)]
    lane = lax.broadcasted_iota(jnp.int32, flat, 1)
    slope = jnp.where(lane < 3, wx * (-cx * HALF), jnp.where(lane < 6, wy * (-cy * HALF), wz * -HALF))
    fixed = jnp.where(lane < 9, slope, wz * (0.5 * HALF) + bias)
    along_x = jnp.where(lane < 9, 0.0, wx)
    along_y = jnp.where(lane < 9, 0.0, wy)
    shape = (count, rows, 128)
    row = lax.broadcasted_iota(jnp.int32, shape, 1)
    lane = lax.broadcasted_iota(jnp.int32, shape, 2)
    at_x = ((row % xr).astype(f32) + 0.5) * HALF
    at_y = ((row // xr).astype(f32) + 0.5) * HALF
    value = fixed[:, None, :] + (at_x * along_x[:, None, :] + at_y * along_y[:, None, :])
    high = value.astype(bf16).astype(f32)
    middle = (value - high).astype(bf16).astype(f32)
    low = value - high - middle
    part = lane % 3
    table = jnp.where(part == 0, high, jnp.where(part == 1, middle, low))
    return jnp.where(lane < 12, table, 0.0).astype(bf16).reshape(count * rows, 128)


def tile_geometry(offset_rows, table, cx, cy, near_ref, base_ref):
    xr = cx // 2
    gj = max(1, 8 // xr)
    rows = gj * xr
    points = offset_rows.shape[1]
    one = jnp.ones((3, points), f32)
    parts = [offset_rows[k : k + 1] for k in range(3) for _ in range(3)] + [one]
    parts = parts + [jnp.zeros((128 - 12, points), f32)]
    base_ref[...] = dot(table, jnp.concatenate(parts, 0).astype(bf16))
    row = lax.broadcasted_iota(jnp.int32, (rows, points), 0)
    dx = ((row % xr).astype(f32) + 0.5 - cx * offset_rows[0:1]) * HALF
    dy = ((row // xr).astype(f32) + 0.5 - cy * offset_rows[1:2]) * HALF
    dz = (0.5 - offset_rows[2:3]) * HALF
    for side in range(2):
        dxs = dx + side * xr * HALF
        for group in range(cy // gj):
            dys = dy + group * gj * HALF
            start = (side * (cy // gj) + group) * rows
            close = jnp.exp(-0.5 * (dxs * dxs + dys * dys + dz * dz)) * ROOT
            near_ref[start : start + rows, :] = close


def hidden(near_ref, base_ref, w_ref, h, cx, cy):
    xr = cx // 2
    gj = max(1, 8 // xr)
    rows = gj * xr
    base = base_ref[pl.ds(pl.multiple_of(h * rows, rows), rows), :]
    step = jnp.full(base.shape, w_ref[1, h] * (gj * HALF * ROOT), f32)
    places = []
    for side in range(2):
        place = base if side == 0 else base + w_ref[0, h] * (xr * HALF * ROOT)
        for group in range(cy // gj):
            if group:
                place = place + step
            places.append(place)
    u = jnp.concatenate(places, 0)
    t = u * near_ref[...]
    return (t + t * lax.erf(u)).astype(bf16)


def offset_rows(offs_ref, block):
    return jnp.concatenate([offs_ref[a, pl.ds(block, 1), :] for a in range(3)], 0)


def encoder_body(
    cx, cy, cap, t_ref, z_ref, ws_ref, w_ref, b_ref, offs_ref, feats_ref, out_w_ref,
    pay_ref, slot_ref, places_ref, table_ref, wrow_ref, rhs_ref, near_ref, base_ref, even_ref, odd_ref,
):
    step = pl.program_id(0)
    blocks = t_ref.shape[0]
    cells = cx * cy
    rows = cells // 2
    channels, points = feats_ref.shape[1:]
    lanes = 2 * channels
    group = even_ref.shape[0]
    count = wrow_ref.shape[0] * group

    @pl.when(step == 0)
    def _():
        pay_ref[...] = jnp.zeros(pay_ref.shape, bf16)
        rhs_ref[...] = jnp.zeros(rhs_ref.shape, bf16)
        places_ref[...] = offs_ref[...].astype(f32)
        table_ref[...] = weight_table(w_ref, b_ref, cx, cy)
        out_w = out_w_ref[...].astype(f32)
        wrow_ref[...] = jnp.concatenate([out_w, out_w], 1).reshape(wrow_ref.shape)
        row = lax.broadcasted_iota(jnp.int32, (PLANE_ROWS, lanes), 0)
        for b in range(blocks):
            target = t_ref[b]
            rank = jnp.int32(0)
            for other in range(b):
                rank = rank + (t_ref[other] == target).astype(jnp.int32)
            slot_ref[b] = target * cap + rank
            here = pl.ds(cap * rows, PLANE_ROWS)
            old = pay_ref[target, here, :].astype(f32)
            pay_ref[target, here, :] = jnp.where(row == rank, z_ref[b].astype(f32), old).astype(bf16)

    for q in range(2):
        rhs_ref[q * channels : (q + 1) * channels, q * points : (q + 1) * points] = feats_ref[q]
        offset = offset_rows(places_ref, 2 * step + q)
        tile_geometry(offset, table_ref[...], cx, cy, near_ref.at[q], base_ref.at[q])

    def fill(ref, first):
        for i in range(group):
            for q in range(2):
                ref[i, q] = hidden(near_ref.at[q], base_ref.at[q], ws_ref, first + i, cx, cy)

    def drain(ref, index, total):
        left = jnp.concatenate([ref[:, q].reshape(group * cells, points) for q in range(2)], 1)
        out = dot_rows(left, rhs_ref[...])
        weights = wrow_ref[index]
        for i in range(group):
            total = total + out[i * cells : (i + 1) * cells] * weights[i : i + 1]
        return total

    def one(index, total):
        first = 2 * index * group
        fill(odd_ref, first + group)
        total = drain(even_ref, 2 * index, total)
        fill(even_ref, first + 2 * group)
        return drain(odd_ref, 2 * index + 1, total)

    pairs = count // group // 2
    fill(even_ref, 0)
    total = lax.fori_loop(0, pairs - 1, one, jnp.zeros((cells, lanes), f32))
    fill(odd_ref, count - group)
    total = drain(even_ref, 2 * pairs - 2, total)
    total = drain(odd_ref, 2 * pairs - 1, total)
    total = total * points**-0.5
    top, bottom = total[:rows], total[rows:]
    left = lane_left((rows, lanes), channels)
    made = (
        jnp.where(left, top, pltpu.roll(bottom, channels, 1)),
        jnp.where(left, pltpu.roll(top, channels, 1), bottom),
    )
    for q in range(2):
        slot = slot_ref[2 * step + q]
        target = slot // cap
        start = pl.multiple_of((slot - target * cap) * rows, rows)
        pay_ref[target, pl.ds(start, rows), :] = made[q].astype(bf16)


def encoder(targets, zstart, weight_in, bias_in, offsets, feats, out_weight, cx, cy, ny, cap):
    blocks, channels, points = feats.shape
    cells = cx * cy
    rows = cells // 2
    count = out_weight.shape[0]
    group = ENCODE_GROUP
    smem = pl.BlockSpec(memory_space=pltpu.SMEM)
    full = lambda a: pl.BlockSpec(a.shape, lambda i: (0,) * a.ndim)
    payload = (ny, cap * rows + PLANE_ROWS, 2 * channels)
    base_rows = count * max(8, cx // 2)
    return pl.pallas_call(
        functools.partial(encoder_body, cx, cy, cap),
        grid=(blocks // 2,),
        in_specs=[
            smem,
            smem,
            smem,
            full(weight_in),
            full(bias_in),
            full(offsets),
            pl.BlockSpec((2, channels, points), lambda i: (i, 0, 0)),
            full(out_weight),
        ],
        out_specs=[pl.BlockSpec(payload, lambda i: (0, 0, 0)), smem],
        out_shape=[
            jax.ShapeDtypeStruct(payload, bf16),
            jax.ShapeDtypeStruct((blocks,), jnp.int32),
        ],
        scratch_shapes=[
            pltpu.VMEM(offsets.shape, f32),
            pltpu.VMEM((base_rows, 128), bf16),
            pltpu.VMEM((count // group, group, 2 * channels), f32),
            pltpu.VMEM((2 * channels, 2 * points), bf16),
            pltpu.VMEM((2, cells, points), f32),
            pltpu.VMEM((2, base_rows, points), f32),
            pltpu.VMEM((group, 2, cells, points), bf16),
            pltpu.VMEM((group, 2, cells, points), bf16),
        ],
        name="encoder",
    )(targets, zstart, weight_in, weight_in, bias_in, offsets, feats, out_weight)


def plane_onehot(planes, cap, width):
    spread, lanes = planes.shape
    slots = spread // PLANE_ROWS * cap
    shape = (slots * width, spread)
    slot = lax.broadcasted_iota(jnp.int32, shape, 0) // width
    source = (slot // cap) * PLANE_ROWS + slot % cap
    pick = (source == lax.broadcasted_iota(jnp.int32, shape, 1)).astype(f32).astype(bf16)
    rows = dot(pick, planes)
    place = lax.broadcasted_iota(jnp.int32, rows.shape, 1).astype(f32)
    return (rows == place).astype(f32).astype(bf16)


def same_row(shape, width):
    return lax.broadcasted_iota(jnp.int32, shape, 0) % width == lax.broadcasted_iota(jnp.int32, shape, 1) % width


def slot_rows(got_ref, cap, rows, group, width):
    parts = []
    for source in range(got_ref.shape[0]):
        for q in range(cap):
            parts.append(got_ref[source, q * rows + group * width : q * rows + (group + 1) * width, :])
    return jnp.concatenate(parts, 0)


def depth_body(cap, rows, width, got_ref, high_ref, low_ref, out_ref):
    lanes = got_ref.shape[2]
    planes = got_ref[:, cap * rows :, :].reshape(-1, lanes)
    onehot = plane_onehot(planes, cap, width)
    shape = (high_ref.shape[0], onehot.shape[0])
    same = same_row(shape, width)
    high = jnp.where(same, dot_rows(high_ref[...], onehot), 0.0).astype(bf16)
    low = jnp.where(same, dot_rows(low_ref[...], onehot), 0.0).astype(bf16)
    modes = out_ref.shape[0]
    for group in range(rows // width):
        right = slot_rows(got_ref, cap, rows, group, width)
        out = dot(high, right) + dot(low, right)
        out_ref[:, group * width : (group + 1) * width, :] = out.astype(bf16).reshape(modes, width, lanes)


def depth(got, table_rows, rows, cap, width):
    lanes = got.shape[2]
    return pl.pallas_call(
        functools.partial(depth_body, cap, rows, width),
        in_specs=vmem(3),
        out_specs=vmem(1)[0],
        out_shape=jax.ShapeDtypeStruct((M, rows, lanes), bf16),
        name="depth_forward",
    )(near(got), *table_rows)


def skip_body(cap, rows, width, xr, got_ref, weight_ref, bias_ref, high_ref, low_ref, out_ref, back_high_ref, back_low_ref):
    lanes = got_ref.shape[2]
    weight = weight_ref[...]
    zero = jnp.zeros_like(weight)
    pair = jnp.concatenate(
        [jnp.concatenate([weight, zero], 1), jnp.concatenate([zero, weight], 1)], 0
    )
    pair_high = pair.astype(bf16)
    pair_low = (pair - pair_high.astype(f32)).astype(bf16)
    bias = jnp.concatenate([bias_ref[...], bias_ref[...]], 1)
    planes = got_ref[:, cap * rows :, :].reshape(-1, lanes)
    onehot = plane_onehot(planes, cap, xr)
    same = same_row(back_high_ref.shape, xr)
    back_high_ref[...] = jnp.where(same, dot_rows(onehot, high_ref[...]), 0.0).astype(bf16)
    back_low_ref[...] = jnp.where(same, dot_rows(onehot, low_ref[...]), 0.0).astype(bf16)
    onehot = plane_onehot(planes, cap, width)
    size = onehot.shape[0]
    same = same_row((size, size), width)
    shared = jnp.where(same, dot_rows(onehot, onehot), 0.0).astype(bf16)
    for group in range(rows // width):
        cells = dot(shared, slot_rows(got_ref, cap, rows, group, width))
        high = cells.astype(bf16)
        low = (cells - high.astype(f32)).astype(bf16)
        term = dot(high, pair_high) + dot(low, pair_high) + dot(high, pair_low) + bias
        out_ref[:, group * width : (group + 1) * width, :] = term.reshape(size // width, width, lanes)


def skip(got, weight, bias, table_rows, rows, cap, width, xr):
    lanes = got.shape[2]
    slots = got.shape[0] * cap
    back = jax.ShapeDtypeStruct((slots * xr, table_rows[0].shape[0]), bf16)
    return pl.pallas_call(
        functools.partial(skip_body, cap, rows, width, xr),
        in_specs=vmem(5),
        out_specs=vmem(3),
        out_shape=[jax.ShapeDtypeStruct((slots, rows, lanes), f32), back, back],
        name="skip",
    )(got, weight, bias, *table_rows)


def rows_of(ref, lead, start, size):
    if size % 16 == 0:
        return ref[lead, start : start + size, :]
    return ref[lead].astype(f32)[start : start + size]


def partner(me, d, count):
    if count & (count - 1) == 0:
        return me ^ d
    return (me + d) % count


def swap_pieces(pieces, axis):
    count = len(pieces)
    moved = [pieces[0]]
    for d in range(1, count):
        pairs = [(i, partner(i, d, count)) for i in range(count)]
        moved.append(lax.ppermute(pieces[d], axis, pairs))
    return moved


def source(me, d, count):
    if count & (count - 1) == 0:
        return me ^ d
    return (me + count - d) % count


def width_body(kb, xr, nx, me_ref, in_ref, high_ref, low_ref, *rest):
    out_refs, scratch = rest[:nx], rest[nx]
    ny, total, lanes = in_ref.shape
    rows = total // kb
    inner = kb * xr
    for k in range(kb):
        right = jnp.concatenate([in_ref[y, k * rows : (k + 1) * rows, :] for y in range(ny)], 0)
        out = dot(high_ref[...], right) + dot(low_ref[...], right)
        for e in range(M):
            scratch[e * inner + k * xr : e * inner + (k + 1) * xr, :] = out[e * xr : (e + 1) * xr]
    size = M * inner // nx
    for d in range(nx):
        start = pl.multiple_of(partner(me_ref[0], d, nx) * size, size)
        out_refs[d][...] = scratch[pl.ds(start, size), :].astype(bf16)


def width_forward(me, data, table, nx, kb, xr):
    lanes = data.shape[2]
    size = M * kb * xr
    return pl.pallas_call(
        functools.partial(width_body, kb, xr, nx),
        in_specs=[pl.BlockSpec(memory_space=pltpu.SMEM)] + vmem(3),
        out_specs=vmem(nx),
        out_shape=[jax.ShapeDtypeStruct((size // nx, lanes), bf16)] * nx,
        scratch_shapes=[pltpu.VMEM((size, lanes), f32)],
        name="width_forward",
    )(me, near(data), *table)


def mix_body(kb, nx, inner, me_ref, *rest):
    in_refs = rest[:nx]
    spec_ref, forward_ref, high_ref, low_ref = rest[nx : nx + 4]
    out_refs = rest[nx + 4 : 2 * nx + 4]
    pick_ref, right_ref, back_ref, modes_ref, mixed_ref = rest[2 * nx + 4 :]
    lanes = in_refs[0].shape[1]
    channels = lanes // 2
    fold = MODE_ROWS // kb
    half = fold * channels
    each = spec_ref.shape[1]
    eb = right_ref.shape[0]
    size = M * MODE_ROWS
    step = pl.program_id(0)

    @pl.when(step == 0)
    def _():
        shape = pick_ref.shape[1:]
        row = lax.broadcasted_iota(jnp.int32, shape, 0) % half
        lane = lax.broadcasted_iota(jnp.int32, shape, 1)
        wanted = row % channels - 2 * (row // channels) - (lane % lanes) // channels
        wanted = wanted - 2 * fold * (lane // lanes)
        for v in range(pick_ref.shape[0]):
            pick_ref[v] = (wanted == 2 * fold * v * (shape[1] // lanes)).astype(f32).astype(bf16)
        for d in range(nx):
            start = pl.multiple_of(source(me_ref[0], d, nx) * inner, inner)
            piece = in_refs[d][...].astype(f32)
            for e in range(eb):
                right_ref[e, pl.ds(start, inner), :] = piece[e * inner : (e + 1) * inner]
        left = lane_left((size, lanes), channels)
        place = (lax.broadcasted_iota(jnp.int32, (size, lanes), 0) % MODE_ROWS) // kb
        side = lax.broadcasted_iota(jnp.int32, (size, lanes), 1) // channels
        masks = [place == 2 * pair + side for pair in range(fold // 2)]
        for first in range(0, eb, each):
            right = jnp.concatenate([right_ref[first + e].astype(bf16) for e in range(each)], 1)
            out = dot(forward_ref[...], jnp.concatenate([right, right], 0))
            for e in range(each):
                here = out[:, e * lanes : (e + 1) * lanes]
                halves = jnp.where(left, here[:size], here[size:])
                halves = halves + pltpu.roll(halves, channels, 1)
                high = halves.astype(bf16).astype(f32)
                low = halves - high
                parts = [jnp.where(mask, part, 0.0) for part in (high, low) for mask in masks]
                modes = jnp.concatenate(parts, 1).astype(bf16)
                modes_ref[first // each, e * size : (e + 1) * size, :] = modes

    totals = [jnp.zeros((M, MODE_ROWS, lanes), f32) for e in range(each)]
    width = pick_ref.shape[2] // lanes
    modes = modes_ref[step]
    for v in range(pick_ref.shape[0]):
        spread = dot(modes, pick_ref[v])
        for w in range(width):
            start = (v * width + w) * MODE_ROWS
            for e in range(each):
                part = spread[e * size : (e + 1) * size, w * lanes : (w + 1) * lanes]
                part = part.reshape(M, MODE_ROWS, lanes)
                totals[e] = totals[e] + part * spec_ref[:, e, start : start + MODE_ROWS, :]
    mixed_ref[step] = jnp.concatenate([total.reshape(size, lanes) for total in totals], 1)

    @pl.when(step == pl.num_programs(0) - 1)
    def _():
        count = nx * inner
        left = lane_left((count, lanes), channels)
        for group in range(eb // each):
            mixed = mixed_ref[group]
            high = mixed.astype(bf16)
            low = (mixed - high.astype(f32)).astype(bf16)
            back = dot(high_ref[...], high) + dot(high_ref[...], low) + dot(low_ref[...], high)
            for e in range(each):
                here = back[:, e * lanes : (e + 1) * lanes]
                here = here + pltpu.roll(here, channels, 1)
                back_ref[group * each + e] = jnp.where(left, here[:count], here[count:])
        for d in range(nx):
            start = pl.multiple_of(partner(me_ref[0], d, nx) * inner, inner)
            for e in range(eb):
                made = back_ref[e, pl.ds(start, inner), :]
                out_refs[d][e * inner : (e + 1) * inner, :] = made.astype(bf16)


def mix(me, pieces, spec, forward, inverse, inner):
    nx = len(pieces)
    total, lanes = pieces[0].shape
    eb, kb, wide = spec.shape[1:]
    chunks = wide // lanes
    spec = spec.reshape(M, eb, kb, chunks, lanes).transpose(0, 1, 3, 2, 4).reshape(M, eb, chunks * kb, lanes)
    full = lambda a: pl.BlockSpec(a.shape, lambda e: (0,) * a.ndim)
    each = 2 if eb % 2 == 0 else 1
    piece = pl.BlockSpec((total, lanes), lambda e: (0, 0))
    channels = lanes // 2
    fold = MODE_ROWS // kb
    return pl.pallas_call(
        functools.partial(mix_body, kb, nx, inner),
        grid=(eb // each,),
        in_specs=[pl.BlockSpec(memory_space=pltpu.SMEM)]
        + vmem(nx)
        + [
            pl.BlockSpec((M, each) + spec.shape[2:], lambda e: (0, e, 0, 0)),
            full(forward),
            full(inverse[0]),
            full(inverse[1]),
        ],
        out_specs=[piece] * nx,
        out_shape=[jax.ShapeDtypeStruct((total, lanes), bf16)] * nx,
        scratch_shapes=[
            pltpu.VMEM((chunks // fold // 2, fold * lanes, 2 * lanes), bf16),
            pltpu.VMEM((eb, nx * inner, lanes), f32),
            pltpu.VMEM((eb, nx * inner, lanes), f32),
            pltpu.VMEM((eb // each, each * M * MODE_ROWS, 2 * fold * channels), bf16),
            pltpu.VMEM((eb // each, M * MODE_ROWS, each * lanes), f32),
        ],
        name="mix",
    )(me, pieces[0], *[near(piece) for piece in pieces[1:]], spec, forward, *inverse)


def width_back_body(kb, xr, nx, me_ref, *rest):
    in_refs = rest[:nx]
    high_ref, low_ref, out_ref, right_ref, made_ref = rest[nx:]
    total, lanes = in_refs[0].shape
    ny = out_ref.shape[0]
    inner = kb * xr
    for d in range(nx):
        start = pl.multiple_of(source(me_ref[0], d, nx) * total, total)
        right_ref[pl.ds(start, total), :] = in_refs[d][...].astype(f32)
    for k in range(kb):
        right = jnp.concatenate(
            [right_ref[e * inner + k * xr : e * inner + (k + 1) * xr, :] for e in range(M)], 0
        ).astype(bf16)
        out = dot(high_ref[...], right) + dot(low_ref[...], right)
        for y in range(G):
            made_ref[y * inner + k * xr : y * inner + (k + 1) * xr, :] = out[y * xr : (y + 1) * xr]
    out_ref[...] = made_ref[...].astype(bf16).reshape(out_ref.shape)


def width_back(me, pieces, table, ny, kb, xr):
    nx = len(pieces)
    lanes = pieces[0].shape[1]
    inner = kb * xr
    return pl.pallas_call(
        functools.partial(width_back_body, kb, xr, nx),
        in_specs=[pl.BlockSpec(memory_space=pltpu.SMEM)] + vmem(nx + 2),
        out_specs=vmem(1)[0],
        out_shape=jax.ShapeDtypeStruct((ny, G // ny * inner, lanes), bf16),
        scratch_shapes=[pltpu.VMEM((M * inner, lanes), f32), pltpu.VMEM((G * inner, lanes), f32)],
        name="width_back",
    )(me, pieces[0], *[near(piece) for piece in pieces[1:]], *table)


def latent_body(inner, xr, in_ref, skip_ref, high_ref, low_ref, out_ref, scratch):
    ny, total, lanes = in_ref.shape
    slots = skip_ref.shape[0]
    for j in range(total // inner):
        right = jnp.concatenate([rows_of(in_ref, t, j * inner, inner) for t in range(ny)], 0).astype(bf16)
        out = (dot(high_ref[...], right) + dot(low_ref[...], right)).reshape(slots, xr, lanes)
        here = slice(j * xr, (j + 1) * xr)
        out = out + skip_ref[:, here, :]
        scratch[:, here, :] = 0.5 * out * (1.0 + lax.erf(out * ROOT))
    out_ref[...] = scratch[...].astype(bf16)


def latent_tiles(data, skipped, back, inner, xr):
    return pl.pallas_call(
        functools.partial(latent_body, inner, xr),
        in_specs=vmem(4),
        out_specs=vmem(1)[0],
        out_shape=jax.ShapeDtypeStruct(skipped.shape, bf16),
        scratch_shapes=[pltpu.VMEM(skipped.shape, f32)],
        name="latent",
    )(near(data), skipped, *back)


STEP = 4
DECODE_GROUP = 64
AHEAD_GROUP = 16
ENCODE_GROUP = 8


def spread_body(out_w_ref, head_ref, wcol_ref, wide_ref):
    count, channels, cells = wcol_ref.shape
    columns = out_w_ref[...].astype(f32).T
    for h in range(count):
        wcol_ref[h] = jnp.broadcast_to(columns[:, h : h + 1], (channels, cells)).astype(bf16)
    wide_ref[...] = jnp.broadcast_to(head_ref[...], (wide_ref.shape[1], channels)).T


def spread(out_weight, head, cells, points):
    count, channels = out_weight.shape
    return pl.pallas_call(
        spread_body,
        in_specs=vmem(2),
        out_specs=vmem(2),
        out_shape=[
            jax.ShapeDtypeStruct((count, channels, cells), bf16),
            jax.ShapeDtypeStruct((channels, points), f32),
        ],
        name="spread",
    )(out_weight, head)


def ahead_body(cx, cy, group, first, ws_ref, w_ref, b_ref, offs_ref, *rest):
    hidden_ref, places_ref, table_ref, near_ref, base_ref = rest[-5:]
    cells = cx * cy
    step = pl.program_id(0)

    @pl.when(step == 0)
    def _():
        places_ref[...] = offs_ref[...].astype(f32)
        table_ref[...] = weight_table(w_ref, b_ref, cx, cy)

    tile_geometry(offset_rows(places_ref, step + first), table_ref[...], cx, cy, near_ref, base_ref)

    def one(index, carry):
        for i in range(group):
            h = index * group + i
            start = pl.multiple_of(h * cells, cells)
            hidden_ref[0, pl.ds(start, cells), :] = hidden(near_ref, base_ref, ws_ref, h, cx, cy)
        return carry

    lax.fori_loop(0, b_ref.shape[1] // group, one, 0)


def ahead(weight_in, bias_in, offsets, cx, cy, first, number, old):
    _, blocks, points = offsets.shape
    cells = cx * cy
    count = bias_in.shape[1]
    full = lambda a: pl.BlockSpec(a.shape, lambda i: (0,) * a.ndim)
    made = (blocks, count * cells, points)
    base_rows = count * max(8, cx // 2)
    return pl.pallas_call(
        functools.partial(ahead_body, cx, cy, AHEAD_GROUP, first),
        grid=(number,),
        in_specs=[pl.BlockSpec(memory_space=pltpu.SMEM), full(weight_in), full(bias_in), full(offsets)]
        + [pl.BlockSpec(memory_space=pl.ANY)] * len(old),
        out_specs=pl.BlockSpec((1,) + made[1:], lambda i: (i + first, 0, 0)),
        out_shape=jax.ShapeDtypeStruct(made, bf16),
        scratch_shapes=[
            pltpu.VMEM(offsets.shape, f32),
            pltpu.VMEM((base_rows, 128), bf16),
            pltpu.VMEM((cells, points), f32),
            pltpu.VMEM((base_rows, points), f32),
        ],
        input_output_aliases={4: 0} if old else {},
        name="ahead",
    )(weight_in, weight_in, bias_in, offsets, *old)


def decoder_body(cells, group, slot_ref, *rest):
    tile_ref, ready_ref, wcol_ref, wide_ref, out_ref = rest
    step = pl.program_id(0)
    count, channels, _ = wcol_ref.shape
    points = ready_ref.shape[2]

    def tile_of(ref):
        tile = ref[...].astype(f32).T
        return jnp.concatenate([tile[:channels], tile[channels:]], 1).astype(bf16)

    tiles = [tile_of(tile_ref.at[slot_ref[STEP * step + q]]) for q in range(STEP)]

    def one(index, totals):
        first = index * group
        start = pl.multiple_of(first * cells, group * cells)
        out = []
        for q in range(STEP):
            folded = jnp.concatenate([tiles[q] * wcol_ref[first + i] for i in range(group)], 1)
            out.append(totals[q] + dot(folded, ready_ref[q, pl.ds(start, group * cells), :]))
        return tuple(out)

    zero = jnp.zeros((channels, points), f32)
    totals = lax.fori_loop(0, count // group, one, (zero,) * STEP)
    for q in range(STEP):
        values = totals[q] * cells**-0.5
        active = 0.5 * values * (1.0 + lax.erf(values * ROOT))
        row = jnp.sum(active * wide_ref[...], axis=0, keepdims=True)
        out_ref[pl.ds(STEP * step + q, 1), :] = row


def decoder(slots, tiles, ready, wcol, wide, cells):
    blocks, _, points = ready.shape
    group = DECODE_GROUP
    full = lambda a: pl.BlockSpec(a.shape, lambda b, s: (0,) * a.ndim)

    return pl.pallas_call(
        functools.partial(decoder_body, cells, group),
        grid_spec=pltpu.PrefetchScalarGridSpec(
            num_scalar_prefetch=1,
            grid=(blocks // STEP,),
            in_specs=vmem(1)
            + [
                pl.BlockSpec((STEP,) + ready.shape[1:], lambda b, s: (b, 0, 0)),
                full(wcol),
                full(wide),
            ],
            out_specs=pl.BlockSpec((blocks, points), lambda b, s: (0, 0)),
        ),
        out_shape=jax.ShapeDtypeStruct((blocks, points), f32),
        name="decoder",
    )(slots, near(tiles), ready, wcol, wide)


def local(
    point_feats,
    offsets,
    targets,
    zstart,
    enc_in,
    enc_bias,
    enc_out,
    dec_in,
    dec_bias,
    dec_out,
    spec_weight,
    local_weight,
    local_bias,
    head_weight,
):
    nx = lax.axis_size("gx")
    ny = lax.axis_size("gy")
    cx = G // nx
    cy = G // ny
    rows = cx * cy // 2
    xr = cx // 2
    kb = M // ny
    inner = kb * xr
    blocks, channels, points = point_feats.shape
    lanes = 2 * channels
    cap = max(2, 2 * blocks // ny)
    fold = MODE_ROWS // kb

    table = real_basis(G, M)
    eye = np.eye
    depth_table = np.zeros((M, lanes))
    depth_table[:, :G] = table
    depth_rows = two_parts(np.repeat(depth_table, 16, 0))
    depth_back_rows = two_parts(np.repeat(depth_table, xr, 0))
    width_table = two_parts(np.kron(table, eye(xr)))
    width_back_table = two_parts(np.kron(table.T, eye(xr)))
    by_x = table.reshape(M, nx, 2, xr)
    copies = np.tile(eye(kb), (fold, 1))
    length_table = np.einsum("aBvr,fk->vafBkr", by_x, copies).reshape(2 * M * MODE_ROWS, nx * inner)
    length_forward = np.concatenate(two_parts(length_table), 1)
    length_back = two_parts(
        np.einsum("aBvr,fk->vBkraf", by_x, copies).reshape(2 * nx * inner, M * MODE_ROWS)
    )

    swap = functools.partial(lax.all_to_all, split_axis=0, concat_axis=0, tiled=True)
    me = lax.axis_index("gx").astype(jnp.int32).reshape(1)
    offs = jnp.transpose(offsets, (1, 0, 2))

    payload, slots = encoder(
        targets[:, 0], zstart, enc_in, enc_bias[None, :], offs, point_feats, enc_out, cx, cy, ny, cap
    )
    third = blocks // 3
    begin = blocks - 2 * third
    made = functools.partial(ahead, dec_in, dec_bias[None, :], offs, cx, cy)
    got = swap(payload, "gy")
    ready = made(0, begin, ())
    got, ready = lax.optimization_barrier((got, ready))
    data = depth(got, depth_rows, rows, cap, 16)
    ready = made(begin, third, (ready,))
    data = swap(data.reshape(ny, kb * rows, lanes), "gy")
    data, ready = lax.optimization_barrier((data, ready))
    wcol, wide = spread(dec_out, head_weight[None, :], cx * cy, points)
    skipped, *back = skip(got, local_weight, local_bias[None, :], depth_back_rows, rows, cap, 16, xr)
    pieces = width_forward(me, data, width_table, nx, kb, xr)
    pieces = swap_pieces(pieces, "gx")
    pieces = mix(me, pieces, spec_weight, length_forward, length_back, inner)
    pieces = swap_pieces(pieces, "gx")
    data = width_back(me, pieces, width_back_table, ny, kb, xr)
    data = swap(data, "gy")
    data, skipped, back, wcol, wide = lax.optimization_barrier((data, skipped, back, wcol, wide))
    tiles = latent_tiles(data, skipped, back, inner, xr)
    ready = made(begin + third, third, (ready,))
    tiles = swap(tiles.reshape(ny, cap * rows, lanes), "gy")
    tiles = tiles.reshape(ny * cap, rows, lanes)
    return decoder(slots, tiles, ready, wcol, wide, cx * cy)


def solution(mesh):
    placed = (
        P(("gx", "gy"), None, None),
        P(("gx", "gy"), None, None),
        P(("gx", "gy"), None),
        P(("gx", "gy")),
        P(),
        P(),
        P(),
        P(),
        P(),
        P(),
        P(None, "gx", "gy", None),
        P(),
        P(),
        P(),
    )
    return jax.shard_map(
        local, mesh=mesh, in_specs=placed, out_specs=P(("gx", "gy"), None), check_vma=False
    )
```

```python
import functools

import jax
import jax.numpy as jnp
import numpy as np
from jax import lax
from jax.experimental import pallas as pl
from jax.experimental.pallas import tpu as pltpu
from jax.sharding import PartitionSpec as P

G = 64
M = 32
HALF = 0.5
ROOT = 0.5**0.5
f32 = jnp.float32
bf16 = jnp.bfloat16
PLANE_ROWS = 16
MODE_ROWS = 8


def real_basis(length, modes):
    half = modes // 2
    places = np.arange(length, dtype=np.float64)[None, :]
    frequency = np.arange(half, dtype=np.float64)[:, None]
    table = np.concatenate(
        [
            np.cos(2.0 * np.pi * frequency * places / length),
            np.sin(2.0 * np.pi * (frequency + 1.0) * places / length),
        ],
        0,
    )
    return table * (2.0 / length) ** 0.5


def two_parts(matrix):
    matrix = np.asarray(matrix, np.float32)
    high = matrix.astype(bf16)
    low = (matrix - high.astype(np.float32)).astype(bf16)
    return high, low


def dot(a, b):
    return jnp.dot(a, b, preferred_element_type=f32)


def dot_rows(a, b):
    return lax.dot_general(a, b, (((1,), (1,)), ((), ())), preferred_element_type=f32)


def vmem(count):
    return [pl.BlockSpec(memory_space=pltpu.VMEM) for _ in range(count)]


def near(array):
    return pltpu.with_memory_space_constraint(array, pltpu.MemorySpace.VMEM)


def lane_left(shape, half):
    return lax.broadcasted_iota(jnp.int32, shape, len(shape) - 1) < half


def weight_table(w_ref, b_ref, cx, cy):
    xr = cx // 2
    rows = max(8, xr)
    weights = jnp.concatenate([w_ref[...], b_ref[...]], 0) * ROOT
    count = weights.shape[1]
    columns = jnp.concatenate([weights, jnp.zeros_like(weights)], 0).T
    flat = (count, 128)
    wx, wy, wz, bias = [jnp.broadcast_to(columns[:, k : k + 1], flat) for k in range(4)]
    lane = lax.broadcasted_iota(jnp.int32, flat, 1)
    slope = jnp.where(lane < 3, wx * (-cx * HALF), jnp.where(lane < 6, wy * (-cy * HALF), wz * -HALF))
    fixed = jnp.where(lane < 9, slope, wz * (0.5 * HALF) + bias)
    along_x = jnp.where(lane < 9, 0.0, wx)
    along_y = jnp.where(lane < 9, 0.0, wy)
    shape = (count, rows, 128)
    row = lax.broadcasted_iota(jnp.int32, shape, 1)
    lane = lax.broadcasted_iota(jnp.int32, shape, 2)
    at_x = ((row % xr).astype(f32) + 0.5) * HALF
    at_y = ((row // xr).astype(f32) + 0.5) * HALF
    value = fixed[:, None, :] + (at_x * along_x[:, None, :] + at_y * along_y[:, None, :])
    high = value.astype(bf16).astype(f32)
    middle = (value - high).astype(bf16).astype(f32)
    low = value - high - middle
    part = lane % 3
    table = jnp.where(part == 0, high, jnp.where(part == 1, middle, low))
    return jnp.where(lane < 12, table, 0.0).astype(bf16).reshape(count * rows, 128)


def tile_geometry(offset_rows, table, cx, cy, near_ref, base_ref):
    xr = cx // 2
    gj = max(1, 8 // xr)
    rows = gj * xr
    points = offset_rows.shape[1]
    one = jnp.ones((3, points), f32)
    parts = [offset_rows[k : k + 1] for k in range(3) for _ in range(3)] + [one]
    parts = parts + [jnp.zeros((128 - 12, points), f32)]
    base_ref[...] = dot(table, jnp.concatenate(parts, 0).astype(bf16))
    row = lax.broadcasted_iota(jnp.int32, (rows, points), 0)
    dx = ((row % xr).astype(f32) + 0.5 - cx * offset_rows[0:1]) * HALF
    dy = ((row // xr).astype(f32) + 0.5 - cy * offset_rows[1:2]) * HALF
    dz = (0.5 - offset_rows[2:3]) * HALF
    for side in range(2):
        dxs = dx + side * xr * HALF
        for group in range(cy // gj):
            dys = dy + group * gj * HALF
            start = (side * (cy // gj) + group) * rows
            close = jnp.exp(-0.5 * (dxs * dxs + dys * dys + dz * dz)) * ROOT
            near_ref[start : start + rows, :] = close


def hidden(near_ref, base_ref, w_ref, h, cx, cy):
    xr = cx // 2
    gj = max(1, 8 // xr)
    rows = gj * xr
    base = base_ref[pl.ds(pl.multiple_of(h * rows, rows), rows), :]
    step = jnp.full(base.shape, w_ref[1, h] * (gj * HALF * ROOT), f32)
    places = []
    for side in range(2):
        place = base if side == 0 else base + w_ref[0, h] * (xr * HALF * ROOT)
        for group in range(cy // gj):
            if group:
                place = place + step
            places.append(place)
    u = jnp.concatenate(places, 0)
    t = u * near_ref[...]
    return (t + t * lax.erf(u)).astype(bf16)


def offset_rows(offs_ref, block):
    return jnp.concatenate([offs_ref[a, pl.ds(block, 1), :] for a in range(3)], 0)


def encoder_body(
    cx, cy, cap, t_ref, z_ref, ws_ref, w_ref, b_ref, offs_ref, feats_ref, out_w_ref,
    pay_ref, slot_ref, places_ref, table_ref, wrow_ref, rhs_ref, near_ref, base_ref, even_ref, odd_ref,
):
    step = pl.program_id(0)
    blocks = t_ref.shape[0]
    cells = cx * cy
    rows = cells // 2
    channels, points = feats_ref.shape[1:]
    lanes = 2 * channels
    group = even_ref.shape[0]
    count = wrow_ref.shape[0] * group

    @pl.when(step == 0)
    def _():
        pay_ref[...] = jnp.zeros(pay_ref.shape, bf16)
        rhs_ref[...] = jnp.zeros(rhs_ref.shape, bf16)
        places_ref[...] = offs_ref[...].astype(f32)
        table_ref[...] = weight_table(w_ref, b_ref, cx, cy)
        out_w = out_w_ref[...].astype(f32)
        wrow_ref[...] = jnp.concatenate([out_w, out_w], 1).reshape(wrow_ref.shape)
        row = lax.broadcasted_iota(jnp.int32, (PLANE_ROWS, lanes), 0)
        for b in range(blocks):
            target = t_ref[b]
            rank = jnp.int32(0)
            for other in range(b):
                rank = rank + (t_ref[other] == target).astype(jnp.int32)
            slot_ref[b] = target * cap + rank
            here = pl.ds(cap * rows, PLANE_ROWS)
            old = pay_ref[target, here, :].astype(f32)
            pay_ref[target, here, :] = jnp.where(row == rank, z_ref[b].astype(f32), old).astype(bf16)

    for q in range(2):
        rhs_ref[q * channels : (q + 1) * channels, q * points : (q + 1) * points] = feats_ref[q]
        offset = offset_rows(places_ref, 2 * step + q)
        tile_geometry(offset, table_ref[...], cx, cy, near_ref.at[q], base_ref.at[q])

    def fill(ref, first):
        for i in range(group):
            for q in range(2):
                ref[i, q] = hidden(near_ref.at[q], base_ref.at[q], ws_ref, first + i, cx, cy)

    def drain(ref, index, total):
        left = jnp.concatenate([ref[:, q].reshape(group * cells, points) for q in range(2)], 1)
        out = dot_rows(left, rhs_ref[...])
        weights = wrow_ref[index]
        for i in range(group):
            total = total + out[i * cells : (i + 1) * cells] * weights[i : i + 1]
        return total

    def one(index, total):
        first = 2 * index * group
        fill(odd_ref, first + group)
        total = drain(even_ref, 2 * index, total)
        fill(even_ref, first + 2 * group)
        return drain(odd_ref, 2 * index + 1, total)

    pairs = count // group // 2
    fill(even_ref, 0)
    total = lax.fori_loop(0, pairs - 1, one, jnp.zeros((cells, lanes), f32))
    fill(odd_ref, count - group)
    total = drain(even_ref, 2 * pairs - 2, total)
    total = drain(odd_ref, 2 * pairs - 1, total)
    total = total * points**-0.5
    top, bottom = total[:rows], total[rows:]
    left = lane_left((rows, lanes), channels)
    made = (
        jnp.where(left, top, pltpu.roll(bottom, channels, 1)),
        jnp.where(left, pltpu.roll(top, channels, 1), bottom),
    )
    for q in range(2):
        slot = slot_ref[2 * step + q]
        target = slot // cap
        start = pl.multiple_of((slot - target * cap) * rows, rows)
        pay_ref[target, pl.ds(start, rows), :] = made[q].astype(bf16)


def encoder(targets, zstart, weight_in, bias_in, offsets, feats, out_weight, cx, cy, ny, cap):
    blocks, channels, points = feats.shape
    cells = cx * cy
    rows = cells // 2
    count = out_weight.shape[0]
    group = ENCODE_GROUP
    smem = pl.BlockSpec(memory_space=pltpu.SMEM)
    full = lambda a: pl.BlockSpec(a.shape, lambda i: (0,) * a.ndim)
    payload = (ny, cap * rows + PLANE_ROWS, 2 * channels)
    base_rows = count * max(8, cx // 2)
    return pl.pallas_call(
        functools.partial(encoder_body, cx, cy, cap),
        grid=(blocks // 2,),
        in_specs=[
            smem,
            smem,
            smem,
            full(weight_in),
            full(bias_in),
            full(offsets),
            pl.BlockSpec((2, channels, points), lambda i: (i, 0, 0)),
            full(out_weight),
        ],
        out_specs=[pl.BlockSpec(payload, lambda i: (0, 0, 0)), smem],
        out_shape=[
            jax.ShapeDtypeStruct(payload, bf16),
            jax.ShapeDtypeStruct((blocks,), jnp.int32),
        ],
        scratch_shapes=[
            pltpu.VMEM(offsets.shape, f32),
            pltpu.VMEM((base_rows, 128), bf16),
            pltpu.VMEM((count // group, group, 2 * channels), f32),
            pltpu.VMEM((2 * channels, 2 * points), bf16),
            pltpu.VMEM((2, cells, points), f32),
            pltpu.VMEM((2, base_rows, points), f32),
            pltpu.VMEM((group, 2, cells, points), bf16),
            pltpu.VMEM((group, 2, cells, points), bf16),
        ],
        name="encoder",
    )(targets, zstart, weight_in, weight_in, bias_in, offsets, feats, out_weight)


def plane_onehot(planes, cap, width):
    spread, lanes = planes.shape
    slots = spread // PLANE_ROWS * cap
    shape = (slots * width, spread)
    slot = lax.broadcasted_iota(jnp.int32, shape, 0) // width
    source = (slot // cap) * PLANE_ROWS + slot % cap
    pick = (source == lax.broadcasted_iota(jnp.int32, shape, 1)).astype(f32).astype(bf16)
    rows = dot(pick, planes)
    place = lax.broadcasted_iota(jnp.int32, rows.shape, 1).astype(f32)
    return (rows == place).astype(f32).astype(bf16)


def same_row(shape, width):
    return lax.broadcasted_iota(jnp.int32, shape, 0) % width == lax.broadcasted_iota(jnp.int32, shape, 1) % width


def slot_rows(got_ref, cap, rows, group, width):
    parts = []
    for source in range(got_ref.shape[0]):
        for q in range(cap):
            parts.append(got_ref[source, q * rows + group * width : q * rows + (group + 1) * width, :])
    return jnp.concatenate(parts, 0)


def paired(count):
    return 2 if count % 2 == 0 else 1


def depth_body(cap, rows, width, got_ref, high_ref, low_ref, out_ref):
    lanes = got_ref.shape[2]
    planes = got_ref[:, cap * rows :, :].reshape(-1, lanes)
    onehot = plane_onehot(planes, cap, width)
    shape = (high_ref.shape[0], onehot.shape[0])
    same = same_row(shape, width)
    high = jnp.where(same, dot_rows(high_ref[...], onehot), 0.0).astype(bf16)
    low = jnp.where(same, dot_rows(low_ref[...], onehot), 0.0).astype(bf16)
    modes = out_ref.shape[0]
    pair = paired(rows // width)
    for first in range(0, rows // width, pair):
        groups = range(first, first + pair)
        right = jnp.concatenate([slot_rows(got_ref, cap, rows, group, width) for group in groups], 1)
        out = (dot(high, right) + dot(low, right)).astype(bf16)
        for group in groups:
            part = out[:, (group - first) * lanes : (group - first + 1) * lanes]
            out_ref[:, group * width : (group + 1) * width, :] = part.reshape(modes, width, lanes)


def depth(got, table_rows, rows, cap, width):
    lanes = got.shape[2]
    return pl.pallas_call(
        functools.partial(depth_body, cap, rows, width),
        in_specs=vmem(3),
        out_specs=vmem(1)[0],
        out_shape=jax.ShapeDtypeStruct((M, rows, lanes), bf16),
        name="depth_forward",
    )(near(got), *table_rows)


def skip_body(cap, rows, width, xr, got_ref, weight_ref, bias_ref, high_ref, low_ref, out_ref, back_high_ref, back_low_ref):
    lanes = got_ref.shape[2]
    weight = weight_ref[...]
    zero = jnp.zeros_like(weight)
    pair = jnp.concatenate(
        [jnp.concatenate([weight, zero], 1), jnp.concatenate([zero, weight], 1)], 0
    )
    pair_high = pair.astype(bf16)
    pair_low = (pair - pair_high.astype(f32)).astype(bf16)
    bias = jnp.concatenate([bias_ref[...], bias_ref[...]], 1)
    planes = got_ref[:, cap * rows :, :].reshape(-1, lanes)
    onehot = plane_onehot(planes, cap, xr)
    same = same_row(back_high_ref.shape, xr)
    back_high_ref[...] = jnp.where(same, dot_rows(onehot, high_ref[...]), 0.0).astype(bf16)
    back_low_ref[...] = jnp.where(same, dot_rows(onehot, low_ref[...]), 0.0).astype(bf16)
    onehot = plane_onehot(planes, cap, width)
    size = onehot.shape[0]
    same = same_row((size, size), width)
    shared = jnp.where(same, dot_rows(onehot, onehot), 0.0).astype(bf16)
    for group in range(rows // width):
        cells = dot(shared, slot_rows(got_ref, cap, rows, group, width))
        high = cells.astype(bf16)
        low = (cells - high.astype(f32)).astype(bf16)
        term = dot(high, pair_high) + dot(low, pair_high) + dot(high, pair_low) + bias
        out_ref[:, group * width : (group + 1) * width, :] = term.reshape(size // width, width, lanes)


def skip(got, weight, bias, table_rows, rows, cap, width, xr):
    lanes = got.shape[2]
    slots = got.shape[0] * cap
    back = jax.ShapeDtypeStruct((slots * xr, table_rows[0].shape[0]), bf16)
    return pl.pallas_call(
        functools.partial(skip_body, cap, rows, width, xr),
        in_specs=vmem(5),
        out_specs=vmem(3),
        out_shape=[jax.ShapeDtypeStruct((slots, rows, lanes), f32), back, back],
        name="skip",
    )(got, weight, bias, *table_rows)


def rows_of(ref, lead, start, size):
    if size % 16 == 0:
        return ref[lead, start : start + size, :]
    return ref[lead].astype(f32)[start : start + size]


def partner(me, d, count):
    if count & (count - 1) == 0:
        return me ^ d
    return (me + d) % count


def swap_pieces(pieces, axis):
    count = len(pieces)
    moved = [pieces[0]]
    for d in range(1, count):
        pairs = [(i, partner(i, d, count)) for i in range(count)]
        moved.append(lax.ppermute(pieces[d], axis, pairs))
    return moved


def source(me, d, count):
    if count & (count - 1) == 0:
        return me ^ d
    return (me + count - d) % count


def width_body(kb, xr, nx, me_ref, in_ref, high_ref, low_ref, *rest):
    out_refs, scratch = rest[:nx], rest[nx]
    ny, total, lanes = in_ref.shape
    rows = total // kb
    inner = kb * xr
    pair = paired(kb)
    for first in range(0, kb, pair):
        ks = range(first, first + pair)
        right = jnp.concatenate(
            [
                jnp.concatenate([in_ref[y, k * rows : (k + 1) * rows, :] for k in ks], 1)
                for y in range(ny)
            ],
            0,
        )
        out = dot(high_ref[...], right) + dot(low_ref[...], right)
        for k in ks:
            part = out[:, (k - first) * lanes : (k - first + 1) * lanes]
            for e in range(M):
                scratch[e * inner + k * xr : e * inner + (k + 1) * xr, :] = part[e * xr : (e + 1) * xr]
    size = M * inner // nx
    for d in range(nx):
        start = pl.multiple_of(partner(me_ref[0], d, nx) * size, size)
        out_refs[d][...] = scratch[pl.ds(start, size), :].astype(bf16)


def width_forward(me, data, table, nx, kb, xr):
    lanes = data.shape[2]
    size = M * kb * xr
    return pl.pallas_call(
        functools.partial(width_body, kb, xr, nx),
        in_specs=[pl.BlockSpec(memory_space=pltpu.SMEM)] + vmem(3),
        out_specs=vmem(nx),
        out_shape=[jax.ShapeDtypeStruct((size // nx, lanes), bf16)] * nx,
        scratch_shapes=[pltpu.VMEM((size, lanes), f32)],
        name="width_forward",
    )(me, near(data), *table)


def mix_body(kb, nx, inner, me_ref, *rest):
    in_refs = rest[:nx]
    spec_ref, forward_ref, high_ref, low_ref = rest[nx : nx + 4]
    out_refs = rest[nx + 4 : 2 * nx + 4]
    pick_ref, right_ref, back_ref, modes_ref, mixed_ref = rest[2 * nx + 4 :]
    lanes = in_refs[0].shape[1]
    channels = lanes // 2
    fold = MODE_ROWS // kb
    half = fold * channels
    each = spec_ref.shape[1]
    eb = right_ref.shape[0]
    size = M * MODE_ROWS
    step = pl.program_id(0)

    @pl.when(step == 0)
    def _():
        shape = pick_ref.shape[1:]
        row = lax.broadcasted_iota(jnp.int32, shape, 0) % half
        lane = lax.broadcasted_iota(jnp.int32, shape, 1)
        wanted = row % channels - 2 * (row // channels) - (lane % lanes) // channels
        wanted = wanted - 2 * fold * (lane // lanes)
        for v in range(pick_ref.shape[0]):
            pick_ref[v] = (wanted == 2 * fold * v * (shape[1] // lanes)).astype(f32).astype(bf16)
        for d in range(nx):
            start = pl.multiple_of(source(me_ref[0], d, nx) * inner, inner)
            piece = in_refs[d][...].astype(f32)
            for e in range(eb):
                right_ref[e, pl.ds(start, inner), :] = piece[e * inner : (e + 1) * inner]
        left = lane_left((size, lanes), channels)
        place = (lax.broadcasted_iota(jnp.int32, (size, lanes), 0) % MODE_ROWS) // kb
        side = lax.broadcasted_iota(jnp.int32, (size, lanes), 1) // channels
        masks = [place == 2 * pair + side for pair in range(fold // 2)]
        for first in range(0, eb, each):
            right = jnp.concatenate([right_ref[first + e].astype(bf16) for e in range(each)], 1)
            out = dot(forward_ref[...], jnp.concatenate([right, right], 0))
            for e in range(each):
                here = out[:, e * lanes : (e + 1) * lanes]
                halves = jnp.where(left, here[:size], here[size:])
                halves = halves + pltpu.roll(halves, channels, 1)
                high = halves.astype(bf16).astype(f32)
                low = halves - high
                parts = [jnp.where(mask, part, 0.0) for part in (high, low) for mask in masks]
                modes = jnp.concatenate(parts, 1).astype(bf16)
                modes_ref[first // each, e * size : (e + 1) * size, :] = modes

    totals = [jnp.zeros((M, MODE_ROWS, lanes), f32) for e in range(each)]
    width = pick_ref.shape[2] // lanes
    modes = modes_ref[step]
    for v in range(pick_ref.shape[0]):
        spread = dot(modes, pick_ref[v])
        for w in range(width):
            start = (v * width + w) * MODE_ROWS
            for e in range(each):
                part = spread[e * size : (e + 1) * size, w * lanes : (w + 1) * lanes]
                part = part.reshape(M, MODE_ROWS, lanes)
                totals[e] = totals[e] + part * spec_ref[:, e, start : start + MODE_ROWS, :]
    mixed_ref[step] = jnp.concatenate([total.reshape(size, lanes) for total in totals], 1)

    @pl.when(step == pl.num_programs(0) - 1)
    def _():
        count = nx * inner
        left = lane_left((count, lanes), channels)
        for group in range(eb // each):
            mixed = mixed_ref[group]
            high = mixed.astype(bf16)
            low = (mixed - high.astype(f32)).astype(bf16)
            back = dot(high_ref[...], high) + dot(high_ref[...], low) + dot(low_ref[...], high)
            for e in range(each):
                here = back[:, e * lanes : (e + 1) * lanes]
                here = here + pltpu.roll(here, channels, 1)
                back_ref[group * each + e] = jnp.where(left, here[:count], here[count:])
        for d in range(nx):
            start = pl.multiple_of(partner(me_ref[0], d, nx) * inner, inner)
            for e in range(eb):
                made = back_ref[e, pl.ds(start, inner), :]
                out_refs[d][e * inner : (e + 1) * inner, :] = made.astype(bf16)


def mix(me, pieces, spec, forward, inverse, inner):
    nx = len(pieces)
    total, lanes = pieces[0].shape
    eb, kb, wide = spec.shape[1:]
    chunks = wide // lanes
    spec = spec.reshape(M, eb, kb, chunks, lanes).transpose(0, 1, 3, 2, 4).reshape(M, eb, chunks * kb, lanes)
    full = lambda a: pl.BlockSpec(a.shape, lambda e: (0,) * a.ndim)
    each = 2 if eb % 2 == 0 else 1
    piece = pl.BlockSpec((total, lanes), lambda e: (0, 0))
    channels = lanes // 2
    fold = MODE_ROWS // kb
    return pl.pallas_call(
        functools.partial(mix_body, kb, nx, inner),
        grid=(eb // each,),
        in_specs=[pl.BlockSpec(memory_space=pltpu.SMEM)]
        + vmem(nx)
        + [
            pl.BlockSpec((M, each) + spec.shape[2:], lambda e: (0, e, 0, 0)),
            full(forward),
            full(inverse[0]),
            full(inverse[1]),
        ],
        out_specs=[piece] * nx,
        out_shape=[jax.ShapeDtypeStruct((total, lanes), bf16)] * nx,
        scratch_shapes=[
            pltpu.VMEM((chunks // fold // 2, fold * lanes, 2 * lanes), bf16),
            pltpu.VMEM((eb, nx * inner, lanes), f32),
            pltpu.VMEM((eb, nx * inner, lanes), f32),
            pltpu.VMEM((eb // each, each * M * MODE_ROWS, 2 * fold * channels), bf16),
            pltpu.VMEM((eb // each, M * MODE_ROWS, each * lanes), f32),
        ],
        name="mix",
    )(me, pieces[0], *[near(piece) for piece in pieces[1:]], spec, forward, *inverse)


def width_back_body(kb, xr, nx, me_ref, *rest):
    in_refs = rest[:nx]
    high_ref, low_ref, out_ref, right_ref, made_ref = rest[nx:]
    total, lanes = in_refs[0].shape
    ny = out_ref.shape[0]
    inner = kb * xr
    for d in range(nx):
        start = pl.multiple_of(source(me_ref[0], d, nx) * total, total)
        right_ref[pl.ds(start, total), :] = in_refs[d][...].astype(f32)
    pair = paired(kb)
    for first in range(0, kb, pair):
        ks = range(first, first + pair)
        right = jnp.concatenate(
            [
                jnp.concatenate(
                    [right_ref[e * inner + k * xr : e * inner + (k + 1) * xr, :] for e in range(M)], 0
                ).astype(bf16)
                for k in ks
            ],
            1,
        )
        out = dot(high_ref[...], right) + dot(low_ref[...], right)
        for k in ks:
            part = out[:, (k - first) * lanes : (k - first + 1) * lanes]
            for y in range(G):
                made_ref[y * inner + k * xr : y * inner + (k + 1) * xr, :] = part[y * xr : (y + 1) * xr]
    out_ref[...] = made_ref[...].astype(bf16).reshape(out_ref.shape)


def width_back(me, pieces, table, ny, kb, xr):
    nx = len(pieces)
    lanes = pieces[0].shape[1]
    inner = kb * xr
    return pl.pallas_call(
        functools.partial(width_back_body, kb, xr, nx),
        in_specs=[pl.BlockSpec(memory_space=pltpu.SMEM)] + vmem(nx + 2),
        out_specs=vmem(1)[0],
        out_shape=jax.ShapeDtypeStruct((ny, G // ny * inner, lanes), bf16),
        scratch_shapes=[pltpu.VMEM((M * inner, lanes), f32), pltpu.VMEM((G * inner, lanes), f32)],
        name="width_back",
    )(me, pieces[0], *[near(piece) for piece in pieces[1:]], *table)


def latent_body(inner, xr, in_ref, skip_ref, high_ref, low_ref, out_ref, scratch):
    ny, total, lanes = in_ref.shape
    slots = skip_ref.shape[0]
    pair = paired(total // inner)
    for first in range(0, total // inner, pair):
        js = range(first, first + pair)
        right = jnp.concatenate(
            [
                jnp.concatenate([rows_of(in_ref, t, j * inner, inner) for t in range(ny)], 0).astype(bf16)
                for j in js
            ],
            1,
        )
        both = dot(high_ref[...], right) + dot(low_ref[...], right)
        for j in js:
            out = both[:, (j - first) * lanes : (j - first + 1) * lanes].reshape(slots, xr, lanes)
            here = slice(j * xr, (j + 1) * xr)
            out = out + skip_ref[:, here, :]
            scratch[:, here, :] = 0.5 * out * (1.0 + lax.erf(out * ROOT))
    out_ref[...] = scratch[...].astype(bf16)


def latent_tiles(data, skipped, back, inner, xr):
    return pl.pallas_call(
        functools.partial(latent_body, inner, xr),
        in_specs=vmem(4),
        out_specs=vmem(1)[0],
        out_shape=jax.ShapeDtypeStruct(skipped.shape, bf16),
        scratch_shapes=[pltpu.VMEM(skipped.shape, f32)],
        name="latent",
    )(near(data), skipped, *back)


STEP = 4
DECODE_GROUP = 64
AHEAD_GROUP = 16
ENCODE_GROUP = 8


def spread_body(out_w_ref, head_ref, wcol_ref, wide_ref):
    count, channels, cells = wcol_ref.shape
    columns = out_w_ref[...].astype(f32).T
    for h in range(count):
        wcol_ref[h] = jnp.broadcast_to(columns[:, h : h + 1], (channels, cells)).astype(bf16)
    wide_ref[...] = jnp.broadcast_to(head_ref[...], (wide_ref.shape[1], channels)).T


def spread(out_weight, head, cells, points):
    count, channels = out_weight.shape
    return pl.pallas_call(
        spread_body,
        in_specs=vmem(2),
        out_specs=vmem(2),
        out_shape=[
            jax.ShapeDtypeStruct((count, channels, cells), bf16),
            jax.ShapeDtypeStruct((channels, points), f32),
        ],
        name="spread",
    )(out_weight, head)


def ahead_body(cx, cy, group, first, ws_ref, w_ref, b_ref, offs_ref, *rest):
    hidden_ref, places_ref, table_ref, near_ref, base_ref = rest[-5:]
    cells = cx * cy
    step = pl.program_id(0)

    @pl.when(step == 0)
    def _():
        places_ref[...] = offs_ref[...].astype(f32)
        table_ref[...] = weight_table(w_ref, b_ref, cx, cy)

    tile_geometry(offset_rows(places_ref, step + first), table_ref[...], cx, cy, near_ref, base_ref)

    def one(index, carry):
        for i in range(group):
            h = index * group + i
            start = pl.multiple_of(h * cells, cells)
            hidden_ref[0, pl.ds(start, cells), :] = hidden(near_ref, base_ref, ws_ref, h, cx, cy)
        return carry

    lax.fori_loop(0, b_ref.shape[1] // group, one, 0)


def ahead(weight_in, bias_in, offsets, cx, cy, first, number, old):
    _, blocks, points = offsets.shape
    cells = cx * cy
    count = bias_in.shape[1]
    full = lambda a: pl.BlockSpec(a.shape, lambda i: (0,) * a.ndim)
    made = (blocks, count * cells, points)
    base_rows = count * max(8, cx // 2)
    return pl.pallas_call(
        functools.partial(ahead_body, cx, cy, AHEAD_GROUP, first),
        grid=(number,),
        in_specs=[pl.BlockSpec(memory_space=pltpu.SMEM), full(weight_in), full(bias_in), full(offsets)]
        + [pl.BlockSpec(memory_space=pl.ANY)] * len(old),
        out_specs=pl.BlockSpec((1,) + made[1:], lambda i: (i + first, 0, 0)),
        out_shape=jax.ShapeDtypeStruct(made, bf16),
        scratch_shapes=[
            pltpu.VMEM(offsets.shape, f32),
            pltpu.VMEM((base_rows, 128), bf16),
            pltpu.VMEM((cells, points), f32),
            pltpu.VMEM((base_rows, points), f32),
        ],
        input_output_aliases={4: 0} if old else {},
        name="ahead",
    )(weight_in, weight_in, bias_in, offsets, *old)


def decoder_body(cells, group, slot_ref, *rest):
    tile_ref, ready_ref, wcol_ref, wide_ref, out_ref = rest
    step = pl.program_id(0)
    count, channels, _ = wcol_ref.shape
    points = ready_ref.shape[2]

    def tile_of(ref):
        tile = ref[...].astype(f32).T
        return jnp.concatenate([tile[:channels], tile[channels:]], 1).astype(bf16)

    tiles = [tile_of(tile_ref.at[slot_ref[STEP * step + q]]) for q in range(STEP)]

    def one(index, totals):
        first = index * group
        start = pl.multiple_of(first * cells, group * cells)
        out = []
        for q in range(STEP):
            folded = jnp.concatenate([tiles[q] * wcol_ref[first + i] for i in range(group)], 1)
            out.append(totals[q] + dot(folded, ready_ref[q, pl.ds(start, group * cells), :]))
        return tuple(out)

    zero = jnp.zeros((channels, points), f32)
    totals = lax.fori_loop(0, count // group, one, (zero,) * STEP)
    for q in range(STEP):
        values = totals[q] * cells**-0.5
        active = 0.5 * values * (1.0 + lax.erf(values * ROOT))
        row = jnp.sum(active * wide_ref[...], axis=0, keepdims=True)
        out_ref[pl.ds(STEP * step + q, 1), :] = row


def decoder(slots, tiles, ready, wcol, wide, cells):
    blocks, _, points = ready.shape
    group = DECODE_GROUP
    full = lambda a: pl.BlockSpec(a.shape, lambda b, s: (0,) * a.ndim)

    return pl.pallas_call(
        functools.partial(decoder_body, cells, group),
        grid_spec=pltpu.PrefetchScalarGridSpec(
            num_scalar_prefetch=1,
            grid=(blocks // STEP,),
            in_specs=vmem(1)
            + [
                pl.BlockSpec((STEP,) + ready.shape[1:], lambda b, s: (b, 0, 0)),
                full(wcol),
                full(wide),
            ],
            out_specs=pl.BlockSpec((blocks, points), lambda b, s: (0, 0)),
        ),
        out_shape=jax.ShapeDtypeStruct((blocks, points), f32),
        name="decoder",
    )(slots, near(tiles), ready, wcol, wide)


def local(
    point_feats,
    offsets,
    targets,
    zstart,
    enc_in,
    enc_bias,
    enc_out,
    dec_in,
    dec_bias,
    dec_out,
    spec_weight,
    local_weight,
    local_bias,
    head_weight,
):
    nx = lax.axis_size("gx")
    ny = lax.axis_size("gy")
    cx = G // nx
    cy = G // ny
    rows = cx * cy // 2
    xr = cx // 2
    kb = M // ny
    inner = kb * xr
    blocks, channels, points = point_feats.shape
    lanes = 2 * channels
    cap = max(2, 2 * blocks // ny)
    fold = MODE_ROWS // kb

    table = real_basis(G, M)
    eye = np.eye
    depth_table = np.zeros((M, lanes))
    depth_table[:, :G] = table
    depth_rows = two_parts(np.repeat(depth_table, 16, 0))
    depth_back_rows = two_parts(np.repeat(depth_table, xr, 0))
    width_table = two_parts(np.kron(table, eye(xr)))
    width_back_table = two_parts(np.kron(table.T, eye(xr)))
    by_x = table.reshape(M, nx, 2, xr)
    copies = np.tile(eye(kb), (fold, 1))
    length_table = np.einsum("aBvr,fk->vafBkr", by_x, copies).reshape(2 * M * MODE_ROWS, nx * inner)
    length_forward = np.concatenate(two_parts(length_table), 1)
    length_back = two_parts(
        np.einsum("aBvr,fk->vBkraf", by_x, copies).reshape(2 * nx * inner, M * MODE_ROWS)
    )

    swap = functools.partial(lax.all_to_all, split_axis=0, concat_axis=0, tiled=True)
    me = lax.axis_index("gx").astype(jnp.int32).reshape(1)
    offs = jnp.transpose(offsets, (1, 0, 2))

    payload, slots = encoder(
        targets[:, 0], zstart, enc_in, enc_bias[None, :], offs, point_feats, enc_out, cx, cy, ny, cap
    )
    third = blocks // 3
    begin = blocks - 2 * third
    made = functools.partial(ahead, dec_in, dec_bias[None, :], offs, cx, cy)
    got = swap(payload, "gy")
    ready = made(0, begin, ())
    got, ready = lax.optimization_barrier((got, ready))
    data = depth(got, depth_rows, rows, cap, 16)
    ready = made(begin, third, (ready,))
    data = swap(data.reshape(ny, kb * rows, lanes), "gy")
    data, ready = lax.optimization_barrier((data, ready))
    wcol, wide = spread(dec_out, head_weight[None, :], cx * cy, points)
    skipped, *back = skip(got, local_weight, local_bias[None, :], depth_back_rows, rows, cap, 16, xr)
    pieces = width_forward(me, data, width_table, nx, kb, xr)
    pieces = swap_pieces(pieces, "gx")
    pieces = mix(me, pieces, spec_weight, length_forward, length_back, inner)
    pieces = swap_pieces(pieces, "gx")
    data = width_back(me, pieces, width_back_table, ny, kb, xr)
    data = swap(data, "gy")
    data, skipped, back, wcol, wide = lax.optimization_barrier((data, skipped, back, wcol, wide))
    tiles = latent_tiles(data, skipped, back, inner, xr)
    ready = made(begin + third, third, (ready,))
    tiles = swap(tiles.reshape(ny, cap * rows, lanes), "gy")
    tiles = tiles.reshape(ny * cap, rows, lanes)
    return decoder(slots, tiles, ready, wcol, wide, cx * cy)


def solution(mesh):
    placed = (
        P(("gx", "gy"), None, None),
        P(("gx", "gy"), None, None),
        P(("gx", "gy"), None),
        P(("gx", "gy")),
        P(),
        P(),
        P(),
        P(),
        P(),
        P(),
        P(None, "gx", "gy", None),
        P(),
        P(),
        P(),
    )
    return jax.shard_map(
        local, mesh=mesh, in_specs=placed, out_specs=P(("gx", "gy"), None), check_vma=False
    )
```

```python
import functools

import jax
import jax.numpy as jnp
import numpy as np
from jax import lax
from jax.experimental import pallas as pl
from jax.experimental.pallas import tpu as pltpu
from jax.sharding import PartitionSpec as P

G = 64
M = 32
HALF = 0.5
ROOT = 0.5**0.5
f32 = jnp.float32
bf16 = jnp.bfloat16
PLANE_ROWS = 16
MODE_ROWS = 8


def real_basis(length, modes):
    half = modes // 2
    places = np.arange(length, dtype=np.float64)[None, :]
    frequency = np.arange(half, dtype=np.float64)[:, None]
    table = np.concatenate(
        [
            np.cos(2.0 * np.pi * frequency * places / length),
            np.sin(2.0 * np.pi * (frequency + 1.0) * places / length),
        ],
        0,
    )
    return table * (2.0 / length) ** 0.5


def two_parts(matrix):
    matrix = np.asarray(matrix, np.float32)
    high = matrix.astype(bf16)
    low = (matrix - high.astype(np.float32)).astype(bf16)
    return high, low


def dot(a, b):
    return jnp.dot(a, b, preferred_element_type=f32)


def dot_rows(a, b):
    return lax.dot_general(a, b, (((1,), (1,)), ((), ())), preferred_element_type=f32)


def vmem(count):
    return [pl.BlockSpec(memory_space=pltpu.VMEM) for _ in range(count)]


def near(array):
    return pltpu.with_memory_space_constraint(array, pltpu.MemorySpace.VMEM)


def lane_left(shape, half):
    return lax.broadcasted_iota(jnp.int32, shape, len(shape) - 1) < half


def weight_table(w_ref, b_ref, cx, cy):
    xr = cx // 2
    rows = max(8, xr)
    weights = jnp.concatenate([w_ref[...], b_ref[...]], 0) * ROOT
    count = weights.shape[1]
    columns = jnp.concatenate([weights, jnp.zeros_like(weights)], 0).T
    flat = (count, 128)
    wx, wy, wz, bias = [jnp.broadcast_to(columns[:, k : k + 1], flat) for k in range(4)]
    lane = lax.broadcasted_iota(jnp.int32, flat, 1)
    slope = jnp.where(lane < 3, wx * (-cx * HALF), jnp.where(lane < 6, wy * (-cy * HALF), wz * -HALF))
    fixed = jnp.where(lane < 9, slope, wz * (0.5 * HALF) + bias)
    along_x = jnp.where(lane < 9, 0.0, wx)
    along_y = jnp.where(lane < 9, 0.0, wy)
    shape = (count, rows, 128)
    row = lax.broadcasted_iota(jnp.int32, shape, 1)
    lane = lax.broadcasted_iota(jnp.int32, shape, 2)
    at_x = ((row % xr).astype(f32) + 0.5) * HALF
    at_y = ((row // xr).astype(f32) + 0.5) * HALF
    value = fixed[:, None, :] + (at_x * along_x[:, None, :] + at_y * along_y[:, None, :])
    high = value.astype(bf16).astype(f32)
    middle = (value - high).astype(bf16).astype(f32)
    low = value - high - middle
    part = lane % 3
    table = jnp.where(part == 0, high, jnp.where(part == 1, middle, low))
    return jnp.where(lane < 12, table, 0.0).astype(bf16).reshape(count * rows, 128)


def tile_geometry(offset_rows, table, cx, cy, near_ref, base_ref):
    xr = cx // 2
    gj = max(1, 8 // xr)
    rows = gj * xr
    points = offset_rows.shape[1]
    one = jnp.ones((3, points), f32)
    parts = [offset_rows[k : k + 1] for k in range(3) for _ in range(3)] + [one]
    parts = parts + [jnp.zeros((128 - 12, points), f32)]
    base_ref[...] = dot(table, jnp.concatenate(parts, 0).astype(bf16))
    row = lax.broadcasted_iota(jnp.int32, (rows, points), 0)
    dx = ((row % xr).astype(f32) + 0.5 - cx * offset_rows[0:1]) * HALF
    dy = ((row // xr).astype(f32) + 0.5 - cy * offset_rows[1:2]) * HALF
    dz = (0.5 - offset_rows[2:3]) * HALF
    for side in range(2):
        dxs = dx + side * xr * HALF
        for group in range(cy // gj):
            dys = dy + group * gj * HALF
            start = (side * (cy // gj) + group) * rows
            close = jnp.exp(-0.5 * (dxs * dxs + dys * dys + dz * dz)) * ROOT
            near_ref[start : start + rows, :] = close


def hidden(near_ref, base_ref, w_ref, h, cx, cy):
    xr = cx // 2
    gj = max(1, 8 // xr)
    rows = gj * xr
    base = base_ref[pl.ds(pl.multiple_of(h * rows, rows), rows), :]
    step = jnp.full(base.shape, w_ref[1, h] * (gj * HALF * ROOT), f32)
    places = []
    for side in range(2):
        place = base if side == 0 else base + w_ref[0, h] * (xr * HALF * ROOT)
        for group in range(cy // gj):
            if group:
                place = place + step
            places.append(place)
    u = jnp.concatenate(places, 0)
    t = u * near_ref[...]
    return (t + t * lax.erf(u)).astype(bf16)


def offset_rows(offs_ref, block):
    return jnp.concatenate([offs_ref[a, pl.ds(block, 1), :] for a in range(3)], 0)


def encoder_body(
    cx, cy, cap, t_ref, z_ref, ws_ref, w_ref, b_ref, offs_ref, feats_ref, out_w_ref,
    pay_ref, slot_ref, places_ref, table_ref, wrow_ref, rhs_ref, near_ref, base_ref, even_ref, odd_ref,
):
    step = pl.program_id(0)
    blocks = t_ref.shape[0]
    cells = cx * cy
    rows = cells // 2
    channels, points = feats_ref.shape[1:]
    lanes = 2 * channels
    group = even_ref.shape[0]
    count = wrow_ref.shape[0] * group

    @pl.when(step == 0)
    def _():
        pay_ref[...] = jnp.zeros(pay_ref.shape, bf16)
        rhs_ref[...] = jnp.zeros(rhs_ref.shape, bf16)
        places_ref[...] = offs_ref[...].astype(f32)
        table_ref[...] = weight_table(w_ref, b_ref, cx, cy)
        out_w = out_w_ref[...].astype(f32)
        wrow_ref[...] = jnp.concatenate([out_w, out_w], 1).reshape(wrow_ref.shape)
        row = lax.broadcasted_iota(jnp.int32, (PLANE_ROWS, lanes), 0)
        for b in range(blocks):
            target = t_ref[b]
            rank = jnp.int32(0)
            for other in range(b):
                rank = rank + (t_ref[other] == target).astype(jnp.int32)
            slot_ref[b] = target * cap + rank
            here = pl.ds(cap * rows, PLANE_ROWS)
            old = pay_ref[target, here, :].astype(f32)
            pay_ref[target, here, :] = jnp.where(row == rank, z_ref[b].astype(f32), old).astype(bf16)

    for q in range(2):
        rhs_ref[q * channels : (q + 1) * channels, q * points : (q + 1) * points] = feats_ref[q]
        offset = offset_rows(places_ref, 2 * step + q)
        tile_geometry(offset, table_ref[...], cx, cy, near_ref.at[q], base_ref.at[q])

    def fill(ref, first):
        for i in range(group):
            for q in range(2):
                ref[i, q] = hidden(near_ref.at[q], base_ref.at[q], ws_ref, first + i, cx, cy)

    def drain(ref, index, total):
        left = jnp.concatenate([ref[:, q].reshape(group * cells, points) for q in range(2)], 1)
        out = dot_rows(left, rhs_ref[...])
        weights = wrow_ref[index]
        for i in range(group):
            total = total + out[i * cells : (i + 1) * cells] * weights[i : i + 1]
        return total

    def one(index, total):
        first = 2 * index * group
        fill(odd_ref, first + group)
        total = drain(even_ref, 2 * index, total)
        fill(even_ref, first + 2 * group)
        return drain(odd_ref, 2 * index + 1, total)

    pairs = count // group // 2
    fill(even_ref, 0)
    total = lax.fori_loop(0, pairs - 1, one, jnp.zeros((cells, lanes), f32))
    fill(odd_ref, count - group)
    total = drain(even_ref, 2 * pairs - 2, total)
    total = drain(odd_ref, 2 * pairs - 1, total)
    total = total * points**-0.5
    top, bottom = total[:rows], total[rows:]
    left = lane_left((rows, lanes), channels)
    made = (
        jnp.where(left, top, pltpu.roll(bottom, channels, 1)),
        jnp.where(left, pltpu.roll(top, channels, 1), bottom),
    )
    for q in range(2):
        slot = slot_ref[2 * step + q]
        target = slot // cap
        start = pl.multiple_of((slot - target * cap) * rows, rows)
        pay_ref[target, pl.ds(start, rows), :] = made[q].astype(bf16)


def encoder(targets, zstart, weight_in, bias_in, offsets, feats, out_weight, cx, cy, ny, cap):
    blocks, channels, points = feats.shape
    cells = cx * cy
    rows = cells // 2
    count = out_weight.shape[0]
    group = ENCODE_GROUP
    smem = pl.BlockSpec(memory_space=pltpu.SMEM)
    full = lambda a: pl.BlockSpec(a.shape, lambda i: (0,) * a.ndim)
    payload = (ny, cap * rows + PLANE_ROWS, 2 * channels)
    base_rows = count * max(8, cx // 2)
    return pl.pallas_call(
        functools.partial(encoder_body, cx, cy, cap),
        grid=(blocks // 2,),
        in_specs=[
            smem,
            smem,
            smem,
            full(weight_in),
            full(bias_in),
            full(offsets),
            pl.BlockSpec((2, channels, points), lambda i: (i, 0, 0)),
            full(out_weight),
        ],
        out_specs=[pl.BlockSpec(payload, lambda i: (0, 0, 0)), smem],
        out_shape=[
            jax.ShapeDtypeStruct(payload, bf16),
            jax.ShapeDtypeStruct((blocks,), jnp.int32),
        ],
        scratch_shapes=[
            pltpu.VMEM(offsets.shape, f32),
            pltpu.VMEM((base_rows, 128), bf16),
            pltpu.VMEM((count // group, group, 2 * channels), f32),
            pltpu.VMEM((2 * channels, 2 * points), bf16),
            pltpu.VMEM((2, cells, points), f32),
            pltpu.VMEM((2, base_rows, points), f32),
            pltpu.VMEM((group, 2, cells, points), bf16),
            pltpu.VMEM((group, 2, cells, points), bf16),
        ],
        name="encoder",
    )(targets, zstart, weight_in, weight_in, bias_in, offsets, feats, out_weight)


def plane_onehot(planes, cap, width):
    spread, lanes = planes.shape
    slots = spread // PLANE_ROWS * cap
    shape = (slots * width, spread)
    slot = lax.broadcasted_iota(jnp.int32, shape, 0) // width
    source = (slot // cap) * PLANE_ROWS + slot % cap
    pick = (source == lax.broadcasted_iota(jnp.int32, shape, 1)).astype(f32).astype(bf16)
    rows = dot(pick, planes)
    place = lax.broadcasted_iota(jnp.int32, rows.shape, 1).astype(f32)
    return (rows == place).astype(f32).astype(bf16)


def same_row(shape, width):
    return lax.broadcasted_iota(jnp.int32, shape, 0) % width == lax.broadcasted_iota(jnp.int32, shape, 1) % width


def slot_rows(got_ref, cap, rows, group, width):
    parts = []
    for source in range(got_ref.shape[0]):
        for q in range(cap):
            parts.append(got_ref[source, q * rows + group * width : q * rows + (group + 1) * width, :])
    return jnp.concatenate(parts, 0)


def paired(count):
    return 2 if count % 2 == 0 else 1


def depth_body(cap, rows, width, got_ref, high_ref, low_ref, out_ref):
    lanes = got_ref.shape[2]
    planes = got_ref[:, cap * rows :, :].reshape(-1, lanes)
    onehot = plane_onehot(planes, cap, width)
    shape = (high_ref.shape[0], onehot.shape[0])
    same = same_row(shape, width)
    high = jnp.where(same, dot_rows(high_ref[...], onehot), 0.0).astype(bf16)
    low = jnp.where(same, dot_rows(low_ref[...], onehot), 0.0).astype(bf16)
    modes = out_ref.shape[0]
    pair = paired(rows // width)
    for first in range(0, rows // width, pair):
        groups = range(first, first + pair)
        right = jnp.concatenate([slot_rows(got_ref, cap, rows, group, width) for group in groups], 1)
        out = (dot(high, right) + dot(low, right)).astype(bf16)
        for group in groups:
            part = out[:, (group - first) * lanes : (group - first + 1) * lanes]
            out_ref[:, group * width : (group + 1) * width, :] = part.reshape(modes, width, lanes)


def depth(got, table_rows, rows, cap, width):
    lanes = got.shape[2]
    return pl.pallas_call(
        functools.partial(depth_body, cap, rows, width),
        in_specs=vmem(3),
        out_specs=vmem(1)[0],
        out_shape=jax.ShapeDtypeStruct((M, rows, lanes), bf16),
        name="depth_forward",
    )(near(got), *table_rows)


def skip_body(cap, rows, width, xr, got_ref, weight_ref, bias_ref, high_ref, low_ref, out_ref, back_high_ref, back_low_ref):
    lanes = got_ref.shape[2]
    weight = weight_ref[...]
    zero = jnp.zeros_like(weight)
    pair = jnp.concatenate(
        [jnp.concatenate([weight, zero], 1), jnp.concatenate([zero, weight], 1)], 0
    )
    pair_high = pair.astype(bf16)
    pair_low = (pair - pair_high.astype(f32)).astype(bf16)
    bias = jnp.concatenate([bias_ref[...], bias_ref[...]], 1)
    planes = got_ref[:, cap * rows :, :].reshape(-1, lanes)
    onehot = plane_onehot(planes, cap, xr)
    same = same_row(back_high_ref.shape, xr)
    back_high_ref[...] = jnp.where(same, dot_rows(onehot, high_ref[...]), 0.0).astype(bf16)
    back_low_ref[...] = jnp.where(same, dot_rows(onehot, low_ref[...]), 0.0).astype(bf16)
    onehot = plane_onehot(planes, cap, width)
    size = onehot.shape[0]
    same = same_row((size, size), width)
    shared = jnp.where(same, dot_rows(onehot, onehot), 0.0).astype(bf16)
    for group in range(rows // width):
        cells = dot(shared, slot_rows(got_ref, cap, rows, group, width))
        high = cells.astype(bf16)
        low = (cells - high.astype(f32)).astype(bf16)
        term = dot(high, pair_high) + dot(low, pair_high) + dot(high, pair_low) + bias
        out_ref[:, group * width : (group + 1) * width, :] = term.reshape(size // width, width, lanes)


def skip(got, weight, bias, table_rows, rows, cap, width, xr):
    lanes = got.shape[2]
    slots = got.shape[0] * cap
    back = jax.ShapeDtypeStruct((slots * xr, table_rows[0].shape[0]), bf16)
    return pl.pallas_call(
        functools.partial(skip_body, cap, rows, width, xr),
        in_specs=vmem(5),
        out_specs=vmem(3),
        out_shape=[jax.ShapeDtypeStruct((slots, rows, lanes), f32), back, back],
        name="skip",
    )(got, weight, bias, *table_rows)


def rows_of(ref, lead, start, size):
    if size % 16 == 0:
        return ref[lead, start : start + size, :]
    return ref[lead].astype(f32)[start : start + size]


def partner(me, d, count):
    if count & (count - 1) == 0:
        return me ^ ((count - d) % count)
    return (me + d) % count


def swap_pieces(pieces, axis):
    count = len(pieces)
    moved = [pieces[0]]
    for d in range(1, count):
        pairs = [(i, partner(i, d, count)) for i in range(count)]
        moved.append(lax.ppermute(pieces[d], axis, pairs))
    return moved


def source(me, d, count):
    if count & (count - 1) == 0:
        return me ^ ((count - d) % count)
    return (me + count - d) % count


def width_body(kb, xr, nx, me_ref, in_ref, high_ref, low_ref, *rest):
    out_refs, scratch = rest[:nx], rest[nx]
    ny, total, lanes = in_ref.shape
    rows = total // kb
    inner = kb * xr
    pair = paired(kb)
    for first in range(0, kb, pair):
        ks = range(first, first + pair)
        right = jnp.concatenate(
            [
                jnp.concatenate([in_ref[y, k * rows : (k + 1) * rows, :] for k in ks], 1)
                for y in range(ny)
            ],
            0,
        )
        out = dot(high_ref[...], right) + dot(low_ref[...], right)
        for k in ks:
            part = out[:, (k - first) * lanes : (k - first + 1) * lanes]
            for e in range(M):
                scratch[e * inner + k * xr : e * inner + (k + 1) * xr, :] = part[e * xr : (e + 1) * xr]
    size = M * inner // nx
    for d in range(nx):
        start = pl.multiple_of(partner(me_ref[0], d, nx) * size, size)
        out_refs[d][...] = scratch[pl.ds(start, size), :].astype(bf16)


def width_forward(me, data, table, nx, kb, xr):
    lanes = data.shape[2]
    size = M * kb * xr
    return pl.pallas_call(
        functools.partial(width_body, kb, xr, nx),
        in_specs=[pl.BlockSpec(memory_space=pltpu.SMEM)] + vmem(3),
        out_specs=vmem(nx),
        out_shape=[jax.ShapeDtypeStruct((size // nx, lanes), bf16)] * nx,
        scratch_shapes=[pltpu.VMEM((size, lanes), f32)],
        name="width_forward",
    )(me, near(data), *table)


def mix_body(kb, nx, inner, me_ref, *rest):
    in_refs = rest[:nx]
    spec_ref, forward_ref, high_ref, low_ref = rest[nx : nx + 4]
    out_refs = rest[nx + 4 : 2 * nx + 4]
    pick_ref, right_ref, back_ref, modes_ref, mixed_ref = rest[2 * nx + 4 :]
    lanes = in_refs[0].shape[1]
    channels = lanes // 2
    fold = MODE_ROWS // kb
    half = fold * channels
    each = spec_ref.shape[1]
    eb = right_ref.shape[0]
    size = M * MODE_ROWS
    step = pl.program_id(0)

    @pl.when(step == 0)
    def _():
        shape = pick_ref.shape[1:]
        row = lax.broadcasted_iota(jnp.int32, shape, 0) % half
        lane = lax.broadcasted_iota(jnp.int32, shape, 1)
        wanted = row % channels - 2 * (row // channels) - (lane % lanes) // channels
        wanted = wanted - 2 * fold * (lane // lanes)
        for v in range(pick_ref.shape[0]):
            pick_ref[v] = (wanted == 2 * fold * v * (shape[1] // lanes)).astype(f32).astype(bf16)
        for d in range(nx):
            start = pl.multiple_of(source(me_ref[0], d, nx) * inner, inner)
            piece = in_refs[d][...].astype(f32)
            for e in range(eb):
                right_ref[e, pl.ds(start, inner), :] = piece[e * inner : (e + 1) * inner]
        left = lane_left((size, lanes), channels)
        place = (lax.broadcasted_iota(jnp.int32, (size, lanes), 0) % MODE_ROWS) // kb
        side = lax.broadcasted_iota(jnp.int32, (size, lanes), 1) // channels
        masks = [place == 2 * pair + side for pair in range(fold // 2)]
        for first in range(0, eb, each):
            right = jnp.concatenate([right_ref[first + e].astype(bf16) for e in range(each)], 1)
            out = dot(forward_ref[...], jnp.concatenate([right, right], 0))
            for e in range(each):
                here = out[:, e * lanes : (e + 1) * lanes]
                halves = jnp.where(left, here[:size], here[size:])
                halves = halves + pltpu.roll(halves, channels, 1)
                high = halves.astype(bf16).astype(f32)
                low = halves - high
                parts = [jnp.where(mask, part, 0.0) for part in (high, low) for mask in masks]
                modes = jnp.concatenate(parts, 1).astype(bf16)
                modes_ref[first // each, e * size : (e + 1) * size, :] = modes

    totals = [jnp.zeros((M, MODE_ROWS, lanes), f32) for e in range(each)]
    width = pick_ref.shape[2] // lanes
    modes = modes_ref[step]
    for v in range(pick_ref.shape[0]):
        spread = dot(modes, pick_ref[v])
        for w in range(width):
            start = (v * width + w) * MODE_ROWS
            for e in range(each):
                part = spread[e * size : (e + 1) * size, w * lanes : (w + 1) * lanes]
                part = part.reshape(M, MODE_ROWS, lanes)
                totals[e] = totals[e] + part * spec_ref[:, e, start : start + MODE_ROWS, :]
    mixed_ref[step] = jnp.concatenate([total.reshape(size, lanes) for total in totals], 1)

    @pl.when(step == pl.num_programs(0) - 1)
    def _():
        count = nx * inner
        left = lane_left((count, lanes), channels)
        for group in range(eb // each):
            mixed = mixed_ref[group]
            high = mixed.astype(bf16)
            low = (mixed - high.astype(f32)).astype(bf16)
            back = dot(high_ref[...], high) + dot(high_ref[...], low) + dot(low_ref[...], high)
            for e in range(each):
                here = back[:, e * lanes : (e + 1) * lanes]
                here = here + pltpu.roll(here, channels, 1)
                back_ref[group * each + e] = jnp.where(left, here[:count], here[count:])
        for d in range(nx):
            start = pl.multiple_of(partner(me_ref[0], d, nx) * inner, inner)
            for e in range(eb):
                made = back_ref[e, pl.ds(start, inner), :]
                out_refs[d][e * inner : (e + 1) * inner, :] = made.astype(bf16)


def mix(me, pieces, spec, forward, inverse, inner):
    nx = len(pieces)
    total, lanes = pieces[0].shape
    eb, kb, wide = spec.shape[1:]
    chunks = wide // lanes
    spec = spec.reshape(M, eb, kb, chunks, lanes).transpose(0, 1, 3, 2, 4).reshape(M, eb, chunks * kb, lanes)
    full = lambda a: pl.BlockSpec(a.shape, lambda e: (0,) * a.ndim)
    each = 2 if eb % 2 == 0 else 1
    piece = pl.BlockSpec((total, lanes), lambda e: (0, 0))
    channels = lanes // 2
    fold = MODE_ROWS // kb
    return pl.pallas_call(
        functools.partial(mix_body, kb, nx, inner),
        grid=(eb // each,),
        in_specs=[pl.BlockSpec(memory_space=pltpu.SMEM)]
        + vmem(nx)
        + [
            pl.BlockSpec((M, each) + spec.shape[2:], lambda e: (0, e, 0, 0)),
            full(forward),
            full(inverse[0]),
            full(inverse[1]),
        ],
        out_specs=[piece] * nx,
        out_shape=[jax.ShapeDtypeStruct((total, lanes), bf16)] * nx,
        scratch_shapes=[
            pltpu.VMEM((chunks // fold // 2, fold * lanes, 2 * lanes), bf16),
            pltpu.VMEM((eb, nx * inner, lanes), f32),
            pltpu.VMEM((eb, nx * inner, lanes), f32),
            pltpu.VMEM((eb // each, each * M * MODE_ROWS, 2 * fold * channels), bf16),
            pltpu.VMEM((eb // each, M * MODE_ROWS, each * lanes), f32),
        ],
        name="mix",
    )(me, pieces[0], *[near(piece) for piece in pieces[1:]], spec, forward, *inverse)


def width_back_body(kb, xr, nx, me_ref, *rest):
    in_refs = rest[:nx]
    high_ref, low_ref, out_ref, right_ref, made_ref = rest[nx:]
    total, lanes = in_refs[0].shape
    ny = out_ref.shape[0]
    inner = kb * xr
    for d in range(nx):
        start = pl.multiple_of(source(me_ref[0], d, nx) * total, total)
        right_ref[pl.ds(start, total), :] = in_refs[d][...].astype(f32)
    pair = paired(kb)
    for first in range(0, kb, pair):
        ks = range(first, first + pair)
        right = jnp.concatenate(
            [
                jnp.concatenate(
                    [right_ref[e * inner + k * xr : e * inner + (k + 1) * xr, :] for e in range(M)], 0
                ).astype(bf16)
                for k in ks
            ],
            1,
        )
        out = dot(high_ref[...], right) + dot(low_ref[...], right)
        for k in ks:
            part = out[:, (k - first) * lanes : (k - first + 1) * lanes]
            for y in range(G):
                made_ref[y * inner + k * xr : y * inner + (k + 1) * xr, :] = part[y * xr : (y + 1) * xr]
    out_ref[...] = made_ref[...].astype(bf16).reshape(out_ref.shape)


def width_back(me, pieces, table, ny, kb, xr):
    nx = len(pieces)
    lanes = pieces[0].shape[1]
    inner = kb * xr
    return pl.pallas_call(
        functools.partial(width_back_body, kb, xr, nx),
        in_specs=[pl.BlockSpec(memory_space=pltpu.SMEM)] + vmem(nx + 2),
        out_specs=vmem(1)[0],
        out_shape=jax.ShapeDtypeStruct((ny, G // ny * inner, lanes), bf16),
        scratch_shapes=[pltpu.VMEM((M * inner, lanes), f32), pltpu.VMEM((G * inner, lanes), f32)],
        name="width_back",
    )(me, pieces[0], *[near(piece) for piece in pieces[1:]], *table)


def latent_body(inner, xr, in_ref, skip_ref, high_ref, low_ref, out_ref, scratch):
    ny, total, lanes = in_ref.shape
    slots = skip_ref.shape[0]
    pair = paired(total // inner)
    for first in range(0, total // inner, pair):
        js = range(first, first + pair)
        right = jnp.concatenate(
            [
                jnp.concatenate([rows_of(in_ref, t, j * inner, inner) for t in range(ny)], 0).astype(bf16)
                for j in js
            ],
            1,
        )
        both = dot(high_ref[...], right) + dot(low_ref[...], right)
        for j in js:
            out = both[:, (j - first) * lanes : (j - first + 1) * lanes].reshape(slots, xr, lanes)
            here = slice(j * xr, (j + 1) * xr)
            out = out + skip_ref[:, here, :]
            scratch[:, here, :] = 0.5 * out * (1.0 + lax.erf(out * ROOT))
    out_ref[...] = scratch[...].astype(bf16)


def latent_tiles(data, skipped, back, inner, xr):
    return pl.pallas_call(
        functools.partial(latent_body, inner, xr),
        in_specs=vmem(4),
        out_specs=vmem(1)[0],
        out_shape=jax.ShapeDtypeStruct(skipped.shape, bf16),
        scratch_shapes=[pltpu.VMEM(skipped.shape, f32)],
        name="latent",
    )(near(data), skipped, *back)


STEP = 4
DECODE_GROUP = 64
AHEAD_GROUP = 16
ENCODE_GROUP = 8


def spread_body(out_w_ref, head_ref, wcol_ref, wide_ref):
    count, channels, cells = wcol_ref.shape
    columns = out_w_ref[...].astype(f32).T
    for h in range(count):
        wcol_ref[h] = jnp.broadcast_to(columns[:, h : h + 1], (channels, cells)).astype(bf16)
    wide_ref[...] = jnp.broadcast_to(head_ref[...], (wide_ref.shape[1], channels)).T


def spread(out_weight, head, cells, points):
    count, channels = out_weight.shape
    return pl.pallas_call(
        spread_body,
        in_specs=vmem(2),
        out_specs=vmem(2),
        out_shape=[
            jax.ShapeDtypeStruct((count, channels, cells), bf16),
            jax.ShapeDtypeStruct((channels, points), f32),
        ],
        name="spread",
    )(out_weight, head)


def ahead_body(cx, cy, group, first, ws_ref, w_ref, b_ref, offs_ref, *rest):
    hidden_ref, places_ref, table_ref, near_ref, base_ref = rest[-5:]
    cells = cx * cy
    step = pl.program_id(0)

    @pl.when(step == 0)
    def _():
        places_ref[...] = offs_ref[...].astype(f32)
        table_ref[...] = weight_table(w_ref, b_ref, cx, cy)

    tile_geometry(offset_rows(places_ref, step + first), table_ref[...], cx, cy, near_ref, base_ref)

    def one(index, carry):
        for i in range(group):
            h = index * group + i
            start = pl.multiple_of(h * cells, cells)
            hidden_ref[0, pl.ds(start, cells), :] = hidden(near_ref, base_ref, ws_ref, h, cx, cy)
        return carry

    lax.fori_loop(0, b_ref.shape[1] // group, one, 0)


def ahead(weight_in, bias_in, offsets, cx, cy, first, number, old):
    _, blocks, points = offsets.shape
    cells = cx * cy
    count = bias_in.shape[1]
    full = lambda a: pl.BlockSpec(a.shape, lambda i: (0,) * a.ndim)
    made = (blocks, count * cells, points)
    base_rows = count * max(8, cx // 2)
    return pl.pallas_call(
        functools.partial(ahead_body, cx, cy, AHEAD_GROUP, first),
        grid=(number,),
        in_specs=[pl.BlockSpec(memory_space=pltpu.SMEM), full(weight_in), full(bias_in), full(offsets)]
        + [pl.BlockSpec(memory_space=pl.ANY)] * len(old),
        out_specs=pl.BlockSpec((1,) + made[1:], lambda i: (i + first, 0, 0)),
        out_shape=jax.ShapeDtypeStruct(made, bf16),
        scratch_shapes=[
            pltpu.VMEM(offsets.shape, f32),
            pltpu.VMEM((base_rows, 128), bf16),
            pltpu.VMEM((cells, points), f32),
            pltpu.VMEM((base_rows, points), f32),
        ],
        input_output_aliases={4: 0} if old else {},
        name="ahead",
    )(weight_in, weight_in, bias_in, offsets, *old)


def decoder_body(cells, group, slot_ref, *rest):
    tile_ref, ready_ref, wcol_ref, wide_ref, out_ref = rest
    step = pl.program_id(0)
    count, channels, _ = wcol_ref.shape
    points = ready_ref.shape[2]

    def tile_of(ref):
        tile = ref[...].astype(f32).T
        return jnp.concatenate([tile[:channels], tile[channels:]], 1).astype(bf16)

    tiles = [tile_of(tile_ref.at[slot_ref[STEP * step + q]]) for q in range(STEP)]

    def one(index, totals):
        first = index * group
        start = pl.multiple_of(first * cells, group * cells)
        out = []
        for q in range(STEP):
            folded = jnp.concatenate([tiles[q] * wcol_ref[first + i] for i in range(group)], 1)
            out.append(totals[q] + dot(folded, ready_ref[q, pl.ds(start, group * cells), :]))
        return tuple(out)

    zero = jnp.zeros((channels, points), f32)
    totals = lax.fori_loop(0, count // group, one, (zero,) * STEP)
    for q in range(STEP):
        values = totals[q] * cells**-0.5
        active = 0.5 * values * (1.0 + lax.erf(values * ROOT))
        row = jnp.sum(active * wide_ref[...], axis=0, keepdims=True)
        out_ref[pl.ds(STEP * step + q, 1), :] = row


def decoder(slots, tiles, ready, wcol, wide, cells):
    blocks, _, points = ready.shape
    group = DECODE_GROUP
    full = lambda a: pl.BlockSpec(a.shape, lambda b, s: (0,) * a.ndim)

    return pl.pallas_call(
        functools.partial(decoder_body, cells, group),
        grid_spec=pltpu.PrefetchScalarGridSpec(
            num_scalar_prefetch=1,
            grid=(blocks // STEP,),
            in_specs=vmem(1)
            + [
                pl.BlockSpec((STEP,) + ready.shape[1:], lambda b, s: (b, 0, 0)),
                full(wcol),
                full(wide),
            ],
            out_specs=pl.BlockSpec((blocks, points), lambda b, s: (0, 0)),
        ),
        out_shape=jax.ShapeDtypeStruct((blocks, points), f32),
        name="decoder",
    )(slots, near(tiles), ready, wcol, wide)


def local(
    point_feats,
    offsets,
    targets,
    zstart,
    enc_in,
    enc_bias,
    enc_out,
    dec_in,
    dec_bias,
    dec_out,
    spec_weight,
    local_weight,
    local_bias,
    head_weight,
):
    nx = lax.axis_size("gx")
    ny = lax.axis_size("gy")
    cx = G // nx
    cy = G // ny
    rows = cx * cy // 2
    xr = cx // 2
    kb = M // ny
    inner = kb * xr
    blocks, channels, points = point_feats.shape
    lanes = 2 * channels
    cap = max(2, 2 * blocks // ny)
    fold = MODE_ROWS // kb

    table = real_basis(G, M)
    eye = np.eye
    depth_table = np.zeros((M, lanes))
    depth_table[:, :G] = table
    depth_rows = two_parts(np.repeat(depth_table, 16, 0))
    depth_back_rows = two_parts(np.repeat(depth_table, xr, 0))
    width_table = two_parts(np.kron(table, eye(xr)))
    width_back_table = two_parts(np.kron(table.T, eye(xr)))
    by_x = table.reshape(M, nx, 2, xr)
    copies = np.tile(eye(kb), (fold, 1))
    length_table = np.einsum("aBvr,fk->vafBkr", by_x, copies).reshape(2 * M * MODE_ROWS, nx * inner)
    length_forward = np.concatenate(two_parts(length_table), 1)
    length_back = two_parts(
        np.einsum("aBvr,fk->vBkraf", by_x, copies).reshape(2 * nx * inner, M * MODE_ROWS)
    )

    swap = functools.partial(lax.all_to_all, split_axis=0, concat_axis=0, tiled=True)
    me = lax.axis_index("gx").astype(jnp.int32).reshape(1)
    offs = jnp.transpose(offsets, (1, 0, 2))

    payload, slots = encoder(
        targets[:, 0], zstart, enc_in, enc_bias[None, :], offs, point_feats, enc_out, cx, cy, ny, cap
    )
    third = blocks // 3
    begin = blocks - 2 * third
    made = functools.partial(ahead, dec_in, dec_bias[None, :], offs, cx, cy)
    got = swap(payload, "gy")
    ready = made(0, begin, ())
    got, ready = lax.optimization_barrier((got, ready))
    data = depth(got, depth_rows, rows, cap, 16)
    ready = made(begin, third, (ready,))
    data = swap(data.reshape(ny, kb * rows, lanes), "gy")
    data, ready = lax.optimization_barrier((data, ready))
    wcol, wide = spread(dec_out, head_weight[None, :], cx * cy, points)
    skipped, *back = skip(got, local_weight, local_bias[None, :], depth_back_rows, rows, cap, 16, xr)
    pieces = width_forward(me, data, width_table, nx, kb, xr)
    pieces = swap_pieces(pieces, "gx")
    pieces = mix(me, pieces, spec_weight, length_forward, length_back, inner)
    pieces = swap_pieces(pieces, "gx")
    data = width_back(me, pieces, width_back_table, ny, kb, xr)
    data = swap(data, "gy")
    data, skipped, back, wcol, wide = lax.optimization_barrier((data, skipped, back, wcol, wide))
    tiles = latent_tiles(data, skipped, back, inner, xr)
    ready = made(begin + third, third, (ready,))
    tiles = swap(tiles.reshape(ny, cap * rows, lanes), "gy")
    tiles = tiles.reshape(ny * cap, rows, lanes)
    return decoder(slots, tiles, ready, wcol, wide, cx * cy)


def solution(mesh):
    placed = (
        P(("gx", "gy"), None, None),
        P(("gx", "gy"), None, None),
        P(("gx", "gy"), None),
        P(("gx", "gy")),
        P(),
        P(),
        P(),
        P(),
        P(),
        P(),
        P(None, "gx", "gy", None),
        P(),
        P(),
        P(),
    )
    return jax.shard_map(
        local, mesh=mesh, in_specs=placed, out_specs=P(("gx", "gy"), None), check_vma=False
    )
```
